128 devices in a mesh: dp: 8 (over z_lo, y), tensor: 16 (over z_hi, x, core).
Axes of the slice: x: 4, y: 4, z: 4 (z_hi: 2, z_lo: 2; z = z_hi * 2 + z_lo), core: 2. Of those that a mesh axis runs over, the one named last changes fastest.
Arguments:
- block_input: bfloat16 [16384, 1024], P(('dp', 'tensor')), may hold values from -6 to 6
- segment_ids: int32 [16, 1024], P('dp'), may hold values from 0 to 3, never falling along the last dimension, each value on 1 to 512 neighbouring positions
- qkv_weight: bfloat16 [3, 1024, 1024], P(None, None, 'tensor'), may hold values from -1 to 1
- qv_bias: float32 [2, 1024], P(None, 'tensor'), may hold values from -3 to 3
- out_weight: bfloat16 [1024, 1024], P('tensor'), may hold values from -1.5 to 1.5
- out_bias: float32 [1024], replicated, may hold values from -3 to 3
- norm1_gain: float32 [1024], replicated, may hold values from 0.5 to 1.5
- norm1_bias: float32 [1024], replicated, may hold values from -3 to 3
- up_weight: bfloat16 [1024, 4096], P(None, 'tensor'), may hold values from -0.1875 to 0.1875
- up_bias: float32 [4096], P('tensor'), may hold values from -3 to 3
- down_weight: bfloat16 [4096, 1024], P('tensor'), may hold values from -0.09375 to 0.09375
- down_bias: float32 [1024], replicated, may hold values from -3 to 3
- norm2_gain: float32 [1024], replicated, may hold values from 0.5 to 1.5
- norm2_bias: float32 [1024], replicated, may hold values from -3 to 3
- cotangent: bfloat16 [16384, 1024], P(('dp', 'tensor')), may hold values from -6 to 6
Outputs:
- layer_output: bfloat16 [16384, 1024], P(('dp', 'tensor'))
- input_grad: bfloat16 [16384, 1024], P(('dp', 'tensor'))
- grad_qkv: float32 [3, 1024, 1024], P(None, None, 'tensor')
- grad_qv_bias: float32 [2, 1024], P(None, 'tensor')
- grad_out_proj: float32 [1024, 1024], P('tensor')
- grad_out_bias: float32 [1024], replicated
- grad_gain_one: float32 [1024], replicated
- grad_bias_one: float32 [1024], replicated
- grad_up: float32 [1024, 4096], P(None, 'tensor')
- grad_up_bias: float32 [4096], P('tensor')
- grad_down: float32 [4096, 1024], P('tensor')
- grad_down_bias: float32 [1024], replicated
- grad_gain_two: float32 [1024], replicated
- grad_bias_two: float32 [1024], replicated
The draws below stay inside these ranges and needn't reach their ends.
Inputs may be any that keep to these rules, and one draw needn't show every extreme that they name: `segment_ids`: document numbers never fall along a sequence; each document holds 1 to 512 tokens.
All inputs are finite; a program needn't handle non-finite values.
Results may differ from the reference program's by a relative error of at most 0.023.
The reference program's roundings to bfloat16 on the way count: a program that leaves them out, or rounds other values in their place, can miss the bound.
Values may be sent and summed in bfloat16 or wider, within the bound.
A program may use at most 128 MiB of HBM per device.

```python
import math
import jax
import jax.numpy as jnp
import numpy as np
from jax import lax

D = 1024
HEADS = 16
HEAD_DIM = 64
FF = 4096
SEQ = 1024
DOCS = 4
DOC_MOST = 512
SEQS = 16
TOKENS = 16384


def draw_block_input(key, part):
    return jax.random.truncated_normal(key, -6.0, 6.0, (TOKENS, D), jnp.float32).astype(jnp.bfloat16)


def draw_qkv_weight(key, part):
    base = jax.random.truncated_normal(key, -5.0, 5.0, (3, D, D), jnp.float32) * D ** (-0.5)
    return jnp.clip(base, -1.0, 1.0).astype(jnp.bfloat16)


def block_scale(rng, dims, pieces, smallest, high):
    level = 1.0
    for axis_at, parts in pieces:
        draws = jax.random.uniform(jax.random.fold_in(jax.random.fold_in(rng, 6), axis_at), (parts,), jnp.float32, smallest / len(pieces), high / len(pieces))
        level = level * jnp.repeat(jnp.exp(draws), dims[axis_at] // parts).reshape((-1,) + (1,) * (len(dims) - 1 - axis_at))
    return level


def length_profile(amount, total, reach, skew):
    loads = [(1 << 20) // math.isqrt(grade ** skew) + 1 for grade in range(2, amount + 1)]
    surplus, counts = total - reach - (amount - 1), [1] * (amount - 1)
    while surplus > 0:
        candidates = [i for i in range(amount - 1) if counts[i] < reach]
        mass, budget = sum([loads[i] for i in candidates]), surplus
        for i in candidates:
            addition = min(reach - counts[i], max(1, budget * loads[i] // mass), surplus)
            counts[i] = counts[i] + addition
            surplus = surplus - addition
    return np.array([reach] + counts)


def ragged(key, count, total, limit, lean):
    if count == 2:
        one = jax.random.randint(key, (), max(1, total - limit), min(limit, total - 1) + 1)
        return jnp.stack([one, total - one])
    tallies = jnp.asarray(length_profile(count, total, limit, lean), jnp.int32)
    pairs = (count - 1) // 2
    donor, sink = tallies[1:1 + 2 * pairs:2], tallies[2:2 + 2 * pairs:2]
    slack = jnp.minimum(donor - 1, limit - sink)
    moved = jax.random.randint(jax.random.fold_in(key, 1), (pairs,), 0, 1 << 20) % (slack + 1)
    tallies = tallies.at[1:1 + 2 * pairs:2].set(donor - moved).at[2:2 + 2 * pairs:2].set(sink + moved)
    return tallies[jax.random.permutation(jax.random.fold_in(key, 2), count)]


def bell_draw(own_key, shape, scale, reach, cuts=(), kind=jnp.bfloat16):
    loudness = block_scale(own_key, shape, cuts, -0.22, 0.18) if cuts else 1.0
    result = jax.random.normal(own_key, shape, jnp.float32) * scale * loudness
    return jnp.minimum(jnp.maximum(result, -reach), reach).astype(kind)


def setup_inputs(seed: int = 0) -> dict:
    arg_keys = jax.random.split(jax.random.key(seed), 16)
    block_input = draw_block_input(jax.random.fold_in(arg_keys[15], 71), 0)
    segment_ids = jax.vmap(lambda own: jnp.searchsorted(jnp.cumsum(ragged(own, DOCS, SEQ, DOC_MOST, 1)), jnp.arange(SEQ), side="right"))(jax.random.split(arg_keys[1], SEQS)).reshape((SEQS, SEQ)).astype(jnp.int32)
    qkv_weight = draw_qkv_weight(jax.random.fold_in(arg_keys[15], 71), 0)
    qv_bias = bell_draw(arg_keys[3], (2, D), 0.5, 3.0, ((1, 16),), jnp.float32)
    out_weight = bell_draw(arg_keys[4], (D, D), (D // 64) ** -0.5, 1.5, ((0, 16),))
    out_bias = bell_draw(arg_keys[5], (D,), 0.5, 3.0, (), jnp.float32)
    norm1_gain = jnp.clip(1.0 + 0.1 * jax.random.normal(arg_keys[6], (D,), jnp.float32), 0.5, 1.5)
    norm1_bias = bell_draw(arg_keys[7], (D,), 0.5, 3.0, (), jnp.float32)
    up_weight = bell_draw(arg_keys[8], (D, FF), D ** -0.5, 0.1875, ((1, 16),))
    up_bias = bell_draw(arg_keys[9], (FF,), 0.5, 3.0, ((0, 16),), jnp.float32)
    down_weight = bell_draw(arg_keys[10], (FF, D), FF ** -0.5, 0.09375, ((0, 16),))
    down_bias = bell_draw(arg_keys[11], (D,), 0.5, 3.0, (), jnp.float32)
    norm2_gain = jnp.clip(1.0 + 0.1 * jax.random.normal(arg_keys[12], (D,), jnp.float32), 0.5, 1.5)
    norm2_bias = bell_draw(arg_keys[13], (D,), 0.5, 3.0, (), jnp.float32)
    cotangent = bell_draw(arg_keys[14], (TOKENS, D), 1.0, 6.0, ((0, 128),))
    return {"block_input": block_input, "segment_ids": segment_ids, "qkv_weight": qkv_weight, "qv_bias": qv_bias, "out_weight": out_weight, "out_bias": out_bias, "norm1_gain": norm1_gain, "norm1_bias": norm1_bias, "up_weight": up_weight, "up_bias": up_bias, "down_weight": down_weight, "down_bias": down_bias, "norm2_gain": norm2_gain, "norm2_bias": norm2_bias, "cotangent": cotangent}


EPS = 1e-12
MASKED = -1e+30
ROOT_HALF = 0.7071067811865476
INV_ROOT_TAU = 0.3989422804014327

def layer_norm(rows, gain, shift):
    center = rows - lax.optimization_barrier(jnp.mean(rows, axis=-1, keepdims=True))
    inverse = lax.rsqrt(lax.optimization_barrier(jnp.mean(center * center, axis=-1, keepdims=True)) + EPS)
    normed = center * inverse
    return (normed * gain + shift, normed, inverse)

def norm_back(grad, normed, inverse, gain):
    scaled = grad * gain
    return inverse * (scaled - lax.optimization_barrier(jnp.mean(scaled, axis=-1, keepdims=True)) - normed * lax.optimization_barrier(jnp.mean(scaled * normed, axis=-1, keepdims=True)))

def gelu_parts(pre):
    cumul = 0.5 * (1.0 + lax.erf(pre * ROOT_HALF))
    return (pre * cumul, cumul + pre * jnp.exp(-0.5 * pre * pre) * INV_ROOT_TAU)

def masked_scores(queries, keys, segs):
    scores = jnp.einsum('qhd,khd->hqk', queries.astype(jnp.float32), keys.astype(jnp.float32)) * HEAD_DIM ** (-0.5)
    allowed = segs[:, None] == segs[None, :]
    return jnp.where(allowed[None], scores, MASKED)

def attend(queries, keys, values, segs):
    masked = masked_scores(queries, keys, segs)
    top = lax.optimization_barrier(jnp.max(masked, axis=-1, keepdims=True))
    lse = top + jnp.log(lax.optimization_barrier(jnp.sum(jnp.exp(masked - top), axis=-1, keepdims=True)))
    probs = jnp.exp(masked - lse).astype(jnp.bfloat16)
    context = jnp.einsum('hqk,khd->qhd', probs.astype(jnp.float32), values.astype(jnp.float32))
    return (context.astype(jnp.bfloat16), lse)

def attend_back(queries, keys, values, segs, lse, d_context):
    masked = masked_scores(queries, keys, segs)
    probs = jnp.exp(masked - lse)
    probs_half = probs.astype(jnp.bfloat16)
    d_values = jnp.einsum('hqk,qhd->khd', probs_half.astype(jnp.float32), d_context.astype(jnp.float32))
    d_probs = jnp.einsum('qhd,khd->hqk', d_context.astype(jnp.float32), values.astype(jnp.float32))
    d_scores = probs * (d_probs - lax.optimization_barrier(jnp.sum(probs * d_probs, axis=-1, keepdims=True))) * HEAD_DIM ** (-0.5)
    d_scores = d_scores.astype(jnp.bfloat16).astype(jnp.float32)
    d_queries = jnp.einsum('hqk,khd->qhd', d_scores, keys.astype(jnp.float32))
    d_keys = jnp.einsum('hqk,qhd->khd', d_scores, queries.astype(jnp.float32))
    return (d_queries, d_keys, d_values)

def split_heads(arr):
    return arr.reshape(SEQ, HEADS, HEAD_DIM)

def reference(block_input, segment_ids, qkv_weight, qv_bias, out_weight, out_bias, norm1_gain, norm1_bias, up_weight, up_bias, down_weight, down_bias, norm2_gain, norm2_bias, cotangent):
    inputs = block_input.reshape(SEQS, SEQ, D)
    cots = cotangent.reshape(SEQS, SEQ, D)

    def one_sequence(totals, items):
        rows, segs, cot = items
        proj = [jnp.dot(rows, qkv_weight[slot], preferred_element_type=jnp.float32) for slot in range(3)]
        queries = (proj[0] + qv_bias[0]).astype(jnp.bfloat16)
        keys = proj[1].astype(jnp.bfloat16)
        values = (proj[2] + qv_bias[1]).astype(jnp.bfloat16)
        context, lse = attend(split_heads(queries), split_heads(keys), split_heads(values), segs)
        context = context.reshape(SEQ, D)
        first = rows.astype(jnp.float32) + jnp.dot(context, out_weight, preferred_element_type=jnp.float32) + out_bias
        hidden, normed_one, inverse_one = layer_norm(first, norm1_gain, norm1_bias)
        hidden_half = hidden.astype(jnp.bfloat16)
        pre = jnp.dot(hidden_half, up_weight, preferred_element_type=jnp.float32) + up_bias
        act, slope = gelu_parts(pre)
        act_half = act.astype(jnp.bfloat16)
        second = hidden + jnp.dot(act_half, down_weight, preferred_element_type=jnp.float32) + down_bias
        output, normed_two, inverse_two = layer_norm(second, norm2_gain, norm2_bias)
        grad = cot.astype(jnp.float32)
        g_gain_two = lax.optimization_barrier(jnp.sum(grad * normed_two, axis=0))
        g_bias_two = lax.optimization_barrier(jnp.sum(grad, axis=0))
        d_second = norm_back(grad, normed_two, inverse_two, norm2_gain)
        g_down_bias = lax.optimization_barrier(jnp.sum(d_second, axis=0))
        d_second_half = d_second.astype(jnp.bfloat16)
        g_down = jnp.dot(act_half.T, d_second_half, preferred_element_type=jnp.float32)
        d_pre = jnp.dot(d_second_half, down_weight.T, preferred_element_type=jnp.float32) * slope
        g_up_bias = lax.optimization_barrier(jnp.sum(d_pre, axis=0))
        d_pre_half = d_pre.astype(jnp.bfloat16)
        g_up = jnp.dot(hidden_half.T, d_pre_half, preferred_element_type=jnp.float32)
        d_hidden = d_second + jnp.dot(d_pre_half, up_weight.T, preferred_element_type=jnp.float32)
        g_gain_one = lax.optimization_barrier(jnp.sum(d_hidden * normed_one, axis=0))
        g_bias_one = lax.optimization_barrier(jnp.sum(d_hidden, axis=0))
        d_first = norm_back(d_hidden, normed_one, inverse_one, norm1_gain)
        g_out_bias = lax.optimization_barrier(jnp.sum(d_first, axis=0))
        d_first_half = d_first.astype(jnp.bfloat16)
        g_out = jnp.dot(context.T, d_first_half, preferred_element_type=jnp.float32)
        d_context = jnp.dot(d_first_half, out_weight.T, preferred_element_type=jnp.float32).astype(jnp.bfloat16)
        d_queries, d_keys, d_values = attend_back(split_heads(queries), split_heads(keys), split_heads(values), segs, lse, split_heads(d_context))
        d_queries = d_queries.reshape(SEQ, D)
        d_keys = d_keys.reshape(SEQ, D)
        d_values = d_values.reshape(SEQ, D)
        g_qv_bias = jnp.stack([lax.optimization_barrier(jnp.sum(d_queries, axis=0)), lax.optimization_barrier(jnp.sum(d_values, axis=0))])
        halves = [d_queries.astype(jnp.bfloat16), d_keys.astype(jnp.bfloat16), d_values.astype(jnp.bfloat16)]
        g_qkv = jnp.stack([jnp.dot(rows.T, halves[slot], preferred_element_type=jnp.float32) for slot in range(3)])
        d_input = d_first
        for slot in range(3):
            d_input = d_input + jnp.dot(halves[slot], qkv_weight[slot].T, preferred_element_type=jnp.float32)
        terms = (g_qkv, g_qv_bias, g_out, g_out_bias, g_gain_one, g_bias_one, g_up, g_up_bias, g_down, g_down_bias, g_gain_two, g_bias_two)
        new_totals = tuple((total + term for total, term in zip(totals, terms)))
        return (new_totals, (output.astype(jnp.bfloat16), d_input.astype(jnp.bfloat16)))
    zero_init = (jnp.zeros((3, D, D), jnp.float32), jnp.zeros((2, D), jnp.float32), jnp.zeros((D, D), jnp.float32), jnp.zeros((D,), jnp.float32), jnp.zeros((D,), jnp.float32), jnp.zeros((D,), jnp.float32), jnp.zeros((D, FF), jnp.float32), jnp.zeros((FF,), jnp.float32), jnp.zeros((FF, D), jnp.float32), jnp.zeros((D,), jnp.float32), jnp.zeros((D,), jnp.float32), jnp.zeros((D,), jnp.float32))
    totals, (outputs, grads) = lax.scan(one_sequence, zero_init, (inputs, segment_ids, cots))
    return (outputs.reshape(TOKENS, D), grads.reshape(TOKENS, D), totals[0], totals[1], totals[2], totals[3], totals[4], totals[5], totals[6], totals[7], totals[8], totals[9], totals[10], totals[11])
```

```python
import jax
import jax.numpy as jnp
from jax import lax
from jax.experimental import pallas as pl
from jax.experimental.pallas import tpu as pltpu
from jax.sharding import PartitionSpec as P

HEAD_DIM = 64
RING = 8
BLOCK = 128
HALF = 64
MESH = pl.DeviceIdType.MESH
VMEM_WHOLE = pl.BlockSpec(memory_space=pltpu.VMEM)


EPS = 1e-12
MASKED = -1e30
ROOT_HALF = 0.7071067811865476
INV_ROOT_TAU = 0.3989422804014327


def ring_place():
    t = lax.axis_index("tensor")
    dp = lax.axis_index("dp")
    base = (t // RING) * RING
    j = t % RING
    x = j // 2
    c = j % 2

    def block_of(step, other=False):
        xx = lax.rem(x + step + 4, 4)
        return xx * 2 + ((1 - c) if other else c)

    def device_of(step, other=False):
        return (dp, base + block_of(step, other))

    return j, block_of, device_of


def greet(devices):
    barrier = pltpu.get_barrier_semaphore()
    for device in devices:
        pl.semaphore_signal(barrier, inc=1, device_id=device, device_id_type=MESH)
    pl.semaphore_wait(barrier, len(devices))


def remote(src, dst, send, recv, slot, device):
    return pltpu.make_async_remote_copy(
        src_ref=src,
        dst_ref=dst,
        send_sem=send.at[slot],
        recv_sem=recv.at[slot],
        device_id=device,
        device_id_type=MESH,
    )


FIRST = pl.ds(0, HALF)
SECOND = pl.ds(HALF, HALF)


def gather_kernel(x_ref, o_ref, send, recv):
    j, block_of, device_of = ring_place()
    right, left, partner = device_of(1), device_of(-1), device_of(0, True)
    mine, from_left, from_right, across = block_of(0), block_of(-1), block_of(1), block_of(2)
    greet((right, left, partner))
    o_at = o_ref.at
    ra = remote(x_ref.at[FIRST], o_at[mine, FIRST], send, recv, 0, right)
    lb = remote(x_ref.at[SECOND], o_at[mine, SECOND], send, recv, 3, left)
    rb = remote(x_ref.at[SECOND], o_at[mine, SECOND], send, recv, 1, right)
    la = remote(x_ref.at[FIRST], o_at[mine, FIRST], send, recv, 2, left)
    own = remote(x_ref, o_at[mine], send, recv, 6, partner)
    started = [ra, lb, rb, la, own]
    for copy in started:
        copy.start()
    o_ref[pl.ds(mine, 1)] = x_ref[...].reshape(1, BLOCK, x_ref.shape[1])

    def pass_on(slot, block, half, partner_slot, device=None, device_slot=None):
        arrived = remote(o_at[block, half], o_at[block, half], send, recv, slot, partner)
        arrived.wait_recv()
        if device is not None:
            on = remote(o_at[block, half], o_at[block, half], send, recv, device_slot, device)
            on.start()
            started.append(on)
        share = remote(o_at[block, half], o_at[block, half], send, recv, partner_slot, partner)
        share.start()
        started.append(share)

    pass_on(0, from_left, FIRST, 7, right, 4)
    pass_on(3, from_right, SECOND, 10, left, 5)
    pass_on(1, from_left, SECOND, 8)
    pass_on(2, from_right, FIRST, 9)
    pass_on(4, across, FIRST, 11)
    pass_on(5, across, SECOND, 12)
    other = {
        6: o_at[block_of(0, True)],
        7: o_at[block_of(-1, True), FIRST],
        8: o_at[block_of(-1, True), SECOND],
        9: o_at[block_of(1, True), FIRST],
        10: o_at[block_of(1, True), SECOND],
        11: o_at[block_of(2, True), FIRST],
        12: o_at[block_of(2, True), SECOND],
    }
    for slot, place in other.items():
        remote(place, place, send, recv, slot, partner).wait_recv()
    for copy in started:
        copy.wait_send()


def gather_rows(x):
    rows, width = x.shape
    out = pl.pallas_call(
        gather_kernel,
        out_shape=jax.ShapeDtypeStruct((RING, rows, width), x.dtype),
        in_specs=[VMEM_WHOLE],
        out_specs=VMEM_WHOLE,
        scratch_shapes=[pltpu.SemaphoreType.DMA((13,)), pltpu.SemaphoreType.DMA((13,))],
        compiler_params=pltpu.CompilerParams(collective_id=0, has_side_effects=True),
    )(x)
    return out.reshape(RING * rows, width)


def scatter_kernel(y_ref, o_ref, pair, stage, transit, final, send, recv):
    j, block_of, device_of = ring_place()
    right, left, partner = device_of(1), device_of(-1), device_of(0, True)
    greet((right, left, partner))
    wide = jnp.float32
    started = []

    def go(src, dst, slot, device):
        copy = remote(src, dst, send, recv, slot, device)
        copy.start()
        started.append(copy)

    def arrived(place, slot):
        remote(place, place, send, recv, slot, partner).wait_recv()

    for k in (2, 1, 3, 0):
        go(y_ref.at[block_of(k, True)], pair.at[k], k, partner)

    def chip_sum(k, half):
        return y_ref[block_of(k), half].astype(wide) + pair[k, half].astype(wide)

    arrived(pair.at[2], 2)
    stage[0] = chip_sum(2, FIRST).astype(stage.dtype)
    go(stage.at[0], transit.at[0], 4, right)
    stage[1] = chip_sum(2, SECOND).astype(stage.dtype)
    go(stage.at[1], transit.at[1], 5, left)
    arrived(pair.at[1], 1)
    stage[2] = chip_sum(1, SECOND).astype(stage.dtype)
    go(stage.at[2], final.at[0, 1], 6, right)
    arrived(pair.at[3], 3)
    stage[3] = chip_sum(3, FIRST).astype(stage.dtype)
    go(stage.at[3], final.at[1, 0], 7, left)
    arrived(transit.at[0], 4)
    stage[4] = (chip_sum(1, FIRST) + transit[0].astype(wide)).astype(stage.dtype)
    go(stage.at[4], final.at[0, 0], 8, right)
    arrived(transit.at[1], 5)
    stage[5] = (chip_sum(3, SECOND) + transit[1].astype(wide)).astype(stage.dtype)
    go(stage.at[5], final.at[1, 1], 9, left)
    arrived(pair.at[0], 0)
    arrived(final.at[0, 1], 6)
    arrived(final.at[1, 0], 7)
    arrived(final.at[0, 0], 8)
    arrived(final.at[1, 1], 9)
    for h, half in enumerate((FIRST, SECOND)):
        o_ref[half] = chip_sum(0, half) + final[0, h].astype(wide) + final[1, h].astype(wide)
    for copy in started:
        copy.wait_send()


def scatter_rows(y):
    tokens, width = y.shape
    rows = tokens // RING
    return pl.pallas_call(
        scatter_kernel,
        out_shape=jax.ShapeDtypeStruct((rows, width), jnp.float32),
        in_specs=[VMEM_WHOLE],
        out_specs=VMEM_WHOLE,
        scratch_shapes=[
            pltpu.VMEM((4, rows, width), y.dtype),
            pltpu.VMEM((6, HALF, width), y.dtype),
            pltpu.VMEM((2, HALF, width), y.dtype),
            pltpu.VMEM((2, 2, HALF, width), y.dtype),
            pltpu.SemaphoreType.DMA((10,)),
            pltpu.SemaphoreType.DMA((10,)),
        ],
        compiler_params=pltpu.CompilerParams(collective_id=1, has_side_effects=True),
    )(y.reshape(RING, rows, width))


def layer_norm(rows, gain, shift):
    center = rows - jnp.mean(rows, axis=-1, keepdims=True)
    inverse = lax.rsqrt(jnp.mean(center * center, axis=-1, keepdims=True) + EPS)
    normed = center * inverse
    return (normed * gain + shift, normed, inverse)


def norm_back(grad, normed, inverse, gain):
    scaled = grad * gain
    return inverse * (
        scaled
        - jnp.mean(scaled, axis=-1, keepdims=True)
        - normed * jnp.mean(scaled * normed, axis=-1, keepdims=True)
    )


def gelu_parts(pre):
    cumul = 0.5 * (1.0 + lax.erf(pre * ROOT_HALF))
    return (pre * cumul, cumul + pre * jnp.exp(-0.5 * pre * pre) * INV_ROOT_TAU)


def masked_scores(queries, keys, segs):
    scores = jnp.einsum(
        "qhd,khd->hqk", queries, keys, preferred_element_type=jnp.float32
    ) * HEAD_DIM ** (-0.5)
    allowed = segs[:, None] == segs[None, :]
    return jnp.where(allowed[None], scores, MASKED)


def forward_seq(items):
    queries, keys, values, segs = items
    masked = masked_scores(queries, keys, segs)
    top = jnp.max(masked, axis=-1, keepdims=True)
    lse = top + jnp.log(jnp.sum(jnp.exp(masked - top), axis=-1, keepdims=True))
    probs = jnp.exp(masked - lse).astype(jnp.bfloat16)
    context = jnp.einsum("hqk,khd->qhd", probs, values, preferred_element_type=jnp.float32)
    return (context.astype(jnp.bfloat16), lse)


def backward_seq(items):
    queries, keys, values, segs, lse, d_context = items
    masked = masked_scores(queries, keys, segs)
    probs = jnp.exp(masked - lse)
    probs_half = probs.astype(jnp.bfloat16)
    d_values = jnp.einsum("hqk,qhd->khd", probs_half, d_context, preferred_element_type=jnp.float32)
    d_probs = jnp.einsum("qhd,khd->hqk", d_context, values, preferred_element_type=jnp.float32)
    d_scores = (
        probs * (d_probs - jnp.sum(probs * d_probs, axis=-1, keepdims=True)) * HEAD_DIM ** (-0.5)
    )
    d_scores = d_scores.astype(jnp.bfloat16)
    d_queries = jnp.einsum("hqk,khd->qhd", d_scores, keys, preferred_element_type=jnp.float32)
    d_keys = jnp.einsum("hqk,qhd->khd", d_scores, queries, preferred_element_type=jnp.float32)
    return (d_queries, d_keys, d_values)


def contract_rows(left, right):
    return lax.dot_general(
        left, right, (((0,), (0,)), ((), ())), preferred_element_type=jnp.float32
    )


def contract_cols(left, right):
    return lax.dot_general(
        left, right, (((1,), (1,)), ((), ())), preferred_element_type=jnp.float32
    )


def trade(arr):
    return lax.ppermute(arr, "tensor", [(t, (t + RING) % (2 * RING)) for t in range(2 * RING)])


def per_device(
    block_input,
    segment_ids,
    qkv_weight,
    qv_bias,
    out_weight,
    out_bias,
    norm1_gain,
    norm1_bias,
    up_weight,
    up_bias,
    down_weight,
    down_bias,
    norm2_gain,
    norm2_bias,
    cotangent,
):
    half = jnp.bfloat16
    wide = jnp.float32
    my_seq = lax.axis_index("tensor") // RING
    segs = lax.dynamic_index_in_dim(segment_ids, my_seq, 0, keepdims=False)
    seq_len = segs.shape[0]
    qkv_two = jnp.concatenate([qkv_weight, trade(qkv_weight)], axis=2)
    qv_bias_two = jnp.concatenate([qv_bias, trade(qv_bias)], axis=1)
    out_two = jnp.concatenate([out_weight, trade(out_weight)], axis=0)
    up_two = jnp.concatenate([up_weight, trade(up_weight)], axis=1)
    up_bias_two = jnp.concatenate([up_bias, trade(up_bias)], axis=0)
    down_two = jnp.concatenate([down_weight, trade(down_weight)], axis=0)

    gathered = gather_rows(block_input)
    projected = jnp.einsum("td,cdw->ctw", gathered, qkv_two, preferred_element_type=wide)
    queries = (projected[0] + qv_bias_two[0]).astype(half)
    keys = projected[1].astype(half)
    values = (projected[2] + qv_bias_two[1]).astype(half)
    width = queries.shape[1]

    def by_head(arr):
        return arr.reshape(seq_len, width // HEAD_DIM, HEAD_DIM)

    context, lse = forward_seq((by_head(queries), by_head(keys), by_head(values), segs))
    context = context.reshape(seq_len, width)
    attended = scatter_rows(jnp.dot(context, out_two, preferred_element_type=wide).astype(half))
    first = block_input.astype(wide) + attended + out_bias
    hidden, normed_one, inverse_one = layer_norm(first, norm1_gain, norm1_bias)
    hidden_half = gather_rows(hidden.astype(half))
    pre = jnp.dot(hidden_half, up_two, preferred_element_type=wide) + up_bias_two
    act, slope = gelu_parts(pre)
    act_half = act.astype(half)
    down_sum = scatter_rows(jnp.dot(act_half, down_two, preferred_element_type=wide).astype(half))
    second = hidden + down_sum + down_bias
    output, normed_two, inverse_two = layer_norm(second, norm2_gain, norm2_bias)
    grad = cotangent.astype(wide)
    g_gain_two = jnp.sum(grad * normed_two, axis=0)
    g_bias_two = jnp.sum(grad, axis=0)
    d_second = norm_back(grad, normed_two, inverse_two, norm2_gain)
    g_down_bias = jnp.sum(d_second, axis=0)
    d_second_all = gather_rows(d_second.astype(half))
    g_down = contract_rows(act_half, d_second_all)
    d_pre = contract_cols(d_second_all, down_two) * slope
    g_up_bias = jnp.sum(d_pre, axis=0)
    d_pre_half = d_pre.astype(half)
    g_up = contract_rows(hidden_half, d_pre_half)
    d_hidden = d_second + scatter_rows(contract_cols(d_pre_half, up_two).astype(half))
    g_gain_one = jnp.sum(d_hidden * normed_one, axis=0)
    g_bias_one = jnp.sum(d_hidden, axis=0)
    d_first = norm_back(d_hidden, normed_one, inverse_one, norm1_gain)
    g_out_bias = jnp.sum(d_first, axis=0)
    d_first_all = gather_rows(d_first.astype(half))
    g_out = contract_rows(context, d_first_all)
    d_context = contract_cols(d_first_all, out_two).astype(half)
    d_queries, d_keys, d_values = (
        arr.reshape(seq_len, width)
        for arr in backward_seq(
            (by_head(queries), by_head(keys), by_head(values), segs, lse, by_head(d_context))
        )
    )
    g_qv_bias = jnp.stack([jnp.sum(d_queries, axis=0), jnp.sum(d_values, axis=0)])
    d_qkv = jnp.stack([d_queries, d_keys, d_values]).astype(half)
    g_qkv = jnp.einsum("td,ctw->cdw", gathered, d_qkv, preferred_element_type=wide)
    d_rows = jnp.einsum("ctw,cdw->td", d_qkv, qkv_two, preferred_element_type=wide)
    input_grad = (d_first + scatter_rows(d_rows.astype(half))).astype(half)

    def total(grad_two, axis):
        size = grad_two.shape[axis] // 2
        own = lax.slice_in_dim(grad_two, 0, size, axis=axis)
        other = lax.slice_in_dim(grad_two, size, 2 * size, axis=axis)
        return (own + trade(other.astype(half)).astype(wide)).astype(half)

    early = lax.psum((total(g_up, 1), total(g_down, 0)), "dp")
    late = lax.psum((total(g_qkv, 2), total(g_out, 0)), "dp")
    g_up, g_down, g_qkv, g_out = (arr.astype(wide) for arr in early + late)

    sums = jnp.stack([g_out_bias, g_gain_one, g_bias_one, g_down_bias, g_gain_two, g_bias_two])
    sums = lax.psum(sums, ("dp", "tensor"))

    def total_small(grad_two, axis):
        size = grad_two.shape[axis] // 2
        own = lax.slice_in_dim(grad_two, 0, size, axis=axis)
        other = lax.slice_in_dim(grad_two, size, 2 * size, axis=axis)
        return own + trade(other)

    g_qv_bias, g_up_bias = lax.psum((total_small(g_qv_bias, 1), total_small(g_up_bias, 0)), "dp")
    return (
        output.astype(half),
        input_grad,
        g_qkv,
        g_qv_bias,
        g_out,
        sums[0],
        sums[1],
        sums[2],
        g_up,
        g_up_bias,
        g_down,
        sums[3],
        sums[4],
        sums[5],
    )


def solution(mesh):
    placed = (
        P(("dp", "tensor"), None),
        P("dp", None),
        P(None, None, "tensor"),
        P(None, "tensor"),
        P("tensor", None),
        P(),
        P(),
        P(),
        P(None, "tensor"),
        P("tensor"),
        P("tensor", None),
        P(),
        P(),
        P(),
        P(("dp", "tensor"), None),
    )
    return jax.shard_map(
        per_device,
        mesh=mesh,
        in_specs=placed,
        out_specs=(
            P(("dp", "tensor"), None),
            P(("dp", "tensor"), None),
            P(None, None, "tensor"),
            P(None, "tensor"),
            P("tensor", None),
            P(),
            P(),
            P(),
            P(None, "tensor"),
            P("tensor"),
            P("tensor", None),
            P(),
            P(),
            P(),
        ),
        check_vma=False,
    )
```

```python
import functools

import jax
import jax.numpy as jnp
from jax import lax
from jax.experimental import pallas as pl
from jax.experimental.pallas import tpu as pltpu
from jax.sharding import PartitionSpec as P

HEAD_DIM = 64
RING = 8
BLOCK = 128
HALF = 64
CHIP = 2 * BLOCK
PIECES = 8
MESH = pl.DeviceIdType.MESH
VMEM_WHOLE = pl.BlockSpec(memory_space=pltpu.VMEM)
VMEM_BYTES = 60 * 1024 * 1024
half = jnp.bfloat16
wide = jnp.float32


EPS = 1e-12
MASKED = -1e30
ROOT_HALF = 0.7071067811865476
INV_ROOT_TAU = 0.3989422804014327


def ring_place():
    t = lax.axis_index("tensor")
    dp = lax.axis_index("dp")
    base = (t // RING) * RING
    j = t % RING
    x = j // 2
    c = j % 2

    def block_of(step, other=False):
        xx = lax.rem(x + step + 4, 4)
        return xx * 2 + ((1 - c) if other else c)

    def device_of(step, other=False):
        return (dp, base + block_of(step, other))

    return block_of, device_of


def ring_order(s):
    return s + s // 2 - 2 * (s // 3)


def greet(devices):
    barrier = pltpu.get_barrier_semaphore()
    for device in devices:
        pl.semaphore_signal(barrier, inc=1, device_id=device, device_id_type=MESH)
    pl.semaphore_wait(barrier, len(devices))


def greet_ring():
    _, device_of = ring_place()
    greet((device_of(1), device_of(-1), device_of(0, True)))


def remote(src, dst, send, recv, slot, device):
    return pltpu.make_async_remote_copy(
        src_ref=src,
        dst_ref=dst,
        send_sem=send.at[slot],
        recv_sem=recv.at[slot],
        device_id=device,
        device_id_type=MESH,
    )


FIRST = pl.ds(0, HALF)
SECOND = pl.ds(HALF, HALF)


class Gather:
    slots = 13

    def __init__(self, src, out, send, recv):
        self.src, self.out, self.send, self.recv = src, out, send, recv
        self.block_of, self.device_of = ring_place()
        self.partner = self.device_of(0, True)

    def copy(self, place, slot, device):
        return remote(place, place, self.send, self.recv, slot, device)

    def start(self):
        src, at = self.src, self.out.at
        mine, right, left = self.block_of(0), self.device_of(1), self.device_of(-1)
        for part, slot, device in ((FIRST, 0, right), (SECOND, 3, left), (SECOND, 1, right), (FIRST, 2, left)):
            remote(src.at[part], at[mine, part], self.send, self.recv, slot, device).start()
        remote(src, at[mine], self.send, self.recv, 6, self.partner).start()
        self.out[pl.ds(mine, 1)] = src[...].reshape(1, *src.shape)

    def pass_on(self, slot, step, part, share_slot, device=None, device_slot=None):
        place = self.out.at[self.block_of(step), part]
        self.copy(place, slot, self.partner).wait_recv()
        if device is not None:
            self.copy(place, device_slot, device).start()
        self.copy(place, share_slot, self.partner).start()

    def shared(self, step, slots):
        for slot, part in zip(slots, (FIRST, SECOND)):
            self.copy(self.out.at[self.block_of(step, True), part], slot, self.partner).wait_recv()

    def ready(self, s):
        @pl.when(s == 0)
        def _():
            self.copy(self.out.at[self.block_of(0, True)], 6, self.partner).wait_recv()

        @pl.when(s == 1)
        def _():
            self.pass_on(0, -1, FIRST, 7, self.device_of(1), 4)
            self.pass_on(3, 1, SECOND, 10, self.device_of(-1), 5)
            self.pass_on(2, 1, FIRST, 9)
            self.pass_on(1, -1, SECOND, 8)
            self.shared(1, (9, 10))

        @pl.when(s == 2)
        def _():
            self.shared(-1, (7, 8))

        @pl.when(s == 3)
        def _():
            self.pass_on(4, 2, FIRST, 11)
            self.pass_on(5, 2, SECOND, 12)
            self.shared(2, (11, 12))

    def finish(self):
        half_place = self.out.at[0, FIRST]
        for slot in range(13):
            self.copy(self.out.at[0] if slot == 6 else half_place, slot, self.partner).wait_send()


class Scatter:
    slots = 10

    @staticmethod
    def scratch(width):
        return [
            pltpu.VMEM((RING, BLOCK, width), half),
            pltpu.VMEM((4, BLOCK, width), half),
            pltpu.VMEM((6, HALF, width), half),
            pltpu.VMEM((2, HALF, width), half),
            pltpu.VMEM((2, 2, HALF, width), half),
            pltpu.SemaphoreType.DMA((10,)),
            pltpu.SemaphoreType.DMA((10,)),
        ]

    def __init__(self, y, pair, stage, transit, final, send, recv):
        self.y, self.pair, self.stage, self.transit, self.final = y, pair, stage, transit, final
        self.send, self.recv = send, recv
        self.block_of, self.device_of = ring_place()
        self.partner = self.device_of(0, True)

    def computed(self, k):
        remote(self.y.at[self.block_of(k, True)], self.pair.at[k], self.send, self.recv, k, self.partner).start()

    def arrived(self, place, slot):
        remote(place, place, self.send, self.recv, slot, self.partner).wait_recv()

    def chip_sum(self, k, part):
        return self.y[self.block_of(k), part].astype(wide) + self.pair[k, part].astype(wide)

    def forward(self, at, value, place, slot, device):
        self.stage[at] = value.astype(half)
        remote(self.stage.at[at], place, self.send, self.recv, slot, device).start()

    def sides(self):
        self.arrived(self.pair.at[1], 1)
        self.forward(2, self.chip_sum(1, SECOND), self.final.at[0, 1], 6, self.device_of(1))
        self.arrived(self.pair.at[3], 3)
        self.forward(3, self.chip_sum(3, FIRST), self.final.at[1, 0], 7, self.device_of(-1))

    def across(self):
        self.arrived(self.pair.at[2], 2)
        self.forward(0, self.chip_sum(2, FIRST), self.transit.at[0], 4, self.device_of(1))
        self.forward(1, self.chip_sum(2, SECOND), self.transit.at[1], 5, self.device_of(-1))

    def through(self):
        self.arrived(self.transit.at[0], 4)
        value = self.chip_sum(1, FIRST) + self.transit[0].astype(wide)
        self.forward(4, value, self.final.at[0, 0], 8, self.device_of(1))
        self.arrived(self.transit.at[1], 5)
        value = self.chip_sum(3, SECOND) + self.transit[1].astype(wide)
        self.forward(5, value, self.final.at[1, 1], 9, self.device_of(-1))

    def result(self):
        self.arrived(self.pair.at[0], 0)
        for slot, place in ((6, (0, 1)), (7, (1, 0)), (8, (0, 0)), (9, (1, 1))):
            self.arrived(self.final.at[place], slot)
        final = self.final
        rows = [
            self.chip_sum(0, part) + final[0, h].astype(wide) + final[1, h].astype(wide)
            for h, part in enumerate((FIRST, SECOND))
        ]
        return jnp.concatenate(rows, axis=0)

    def finish(self):
        for slot in range(10):
            place = self.pair.at[0] if slot < 4 else self.transit.at[0]
            remote(place, place, self.send, self.recv, slot, self.partner).wait_send()


def dot_nn(left, right):
    return lax.dot_general(left, right, (((1,), (0,)), ((), ())), preferred_element_type=wide)


def dot_nt(left, right):
    return lax.dot_general(left, right, (((1,), (1,)), ((), ())), preferred_element_type=wide)


def dot_tn(left, right):
    return lax.dot_general(left, right, (((0,), (0,)), ((), ())), preferred_element_type=wide)


def layer_norm(rows, gain, shift):
    center = rows - jnp.mean(rows, axis=-1, keepdims=True)
    inverse = lax.rsqrt(jnp.mean(center * center, axis=-1, keepdims=True) + EPS)
    normed = center * inverse
    return (normed * gain + shift, normed, inverse)


def norm_back(grad, normed, inverse, gain):
    scaled = grad * gain
    return inverse * (
        scaled
        - jnp.mean(scaled, axis=-1, keepdims=True)
        - normed * jnp.mean(scaled * normed, axis=-1, keepdims=True)
    )


def gelu_parts(pre):
    cumul = 0.5 * (1.0 + lax.erf(pre * ROOT_HALF))
    return (pre * cumul, cumul + pre * jnp.exp(-0.5 * pre * pre) * INV_ROOT_TAU)


def column_sum(rows):
    return jnp.sum(rows, axis=0, keepdims=True)


def chip_rows(ref, chip):
    block = ref[pl.ds(2 * chip, 2)]
    return block.reshape(CHIP, block.shape[2])


def all_rows(ref):
    block = ref[...]
    return block.reshape(RING * BLOCK, block.shape[2])


def feed_forward_kernel(
    attended, block_input, out_bias, gain1, bias1, up, up_bias, down, down_bias, gain2, bias2, cot,
    out, d_first, d_first_half, g_up, g_down, g_up_bias, vecs,
    hidden_half, hidden_all, act, slope, d_second_half, d_second_all, d_pre, gather_sems, *scatter_scratch,
):
    block_of, _ = ring_place()
    greet_ring()
    first = block_input[...].astype(wide) + attended[...] + out_bias[...]
    hidden, normed_one, inverse_one = layer_norm(first, gain1[...], bias1[...])
    hidden_half[...] = hidden.astype(half)
    gather = Gather(hidden_half, hidden_all, gather_sems.at[0], gather_sems.at[1])
    scatter = Scatter(*scatter_scratch[:7])
    gather.start()

    @pl.loop(0, 4)
    def _(s):
        gather.ready(s)
        k = ring_order(s)
        chip = block_of(k) // 2
        rows = pl.ds(chip * CHIP, CHIP)
        pre = dot_nn(chip_rows(hidden_all, chip), up[...]) + up_bias[...]
        value, gelu_slope = gelu_parts(pre)
        value = value.astype(half)
        act[rows] = value
        slope[rows] = gelu_slope
        term = dot_nn(value, down[...]).astype(half)
        scatter.y[pl.ds(2 * chip, 2)] = term.reshape(2, BLOCK, term.shape[1])
        scatter.computed(k)

    scatter.sides()
    scatter.across()
    gather.finish()
    scatter.through()
    second = hidden + scatter.result() + down_bias[...]
    scatter.finish()
    output, normed_two, inverse_two = layer_norm(second, gain2[...], bias2[...])
    out[...] = output.astype(half)
    grad = cot[...].astype(wide)
    d_second = norm_back(grad, normed_two, inverse_two, gain2[...])
    d_second_half[...] = d_second.astype(half)
    gather = Gather(d_second_half, d_second_all, gather_sems.at[2], gather_sems.at[3])
    scatter = Scatter(*scatter_scratch[7:])
    gather.start()
    vecs[pl.ds(3, 1)] = column_sum(d_second)
    vecs[pl.ds(4, 1)] = column_sum(grad * normed_two)
    vecs[pl.ds(5, 1)] = column_sum(grad)
    vecs[pl.ds(6, 2)] = jnp.zeros((2, grad.shape[1]), wide)
    g_up_bias[...] = jnp.zeros_like(g_up_bias)

    @pl.loop(0, 4)
    def _(s):
        gather.ready(s)
        k = ring_order(s)
        chip = block_of(k) // 2
        rows = pl.ds(chip * CHIP, CHIP)
        grad_pre = dot_nt(chip_rows(d_second_all, chip), down[...]) * slope[rows]
        g_up_bias[...] += column_sum(grad_pre)
        grad_pre = grad_pre.astype(half)
        d_pre[rows] = grad_pre
        term = dot_nt(grad_pre, up[...]).astype(half)
        scatter.y[pl.ds(2 * chip, 2)] = term.reshape(2, BLOCK, term.shape[1])
        scatter.computed(k)

    scatter.sides()
    scatter.across()
    gather.finish()
    shard = up.shape[1] // 2
    for a in range(2):
        columns = pl.ds(a * shard, shard)
        g_down[a] = dot_tn(act[:, columns], all_rows(d_second_all)).astype(half)
    scatter.through()

    @pl.loop(0, 4)
    def _(i):
        columns = pl.ds(pl.multiple_of(i * 256, 256), 256)
        left = hidden_all[:, :, columns].reshape(RING * BLOCK, 256)
        part = dot_tn(left, d_pre[...]).astype(half)
        for a in range(2):
            g_up[a, columns] = part[:, a * shard : (a + 1) * shard]

    d_hidden = d_second + scatter.result()
    scatter.finish()
    grad_first = norm_back(d_hidden, normed_one, inverse_one, gain1[...])
    d_first[...] = grad_first
    d_first_half[...] = grad_first.astype(half)
    vecs[pl.ds(0, 1)] = column_sum(grad_first)
    vecs[pl.ds(1, 1)] = column_sum(d_hidden * normed_one)
    vecs[pl.ds(2, 1)] = column_sum(d_hidden)


def feed_forward(attended, block_input, out_bias, gain1, bias1, up, up_bias, down, down_bias, gain2, bias2, cot):
    rows, width = attended.shape
    hidden = up.shape[1]
    shard = hidden // 2
    return pl.pallas_call(
        feed_forward_kernel,
        out_shape=(
            jax.ShapeDtypeStruct((rows, width), half),
            jax.ShapeDtypeStruct((rows, width), wide),
            jax.ShapeDtypeStruct((rows, width), half),
            jax.ShapeDtypeStruct((2, width, shard), half),
            jax.ShapeDtypeStruct((2, shard, width), half),
            jax.ShapeDtypeStruct((1, hidden), wide),
            jax.ShapeDtypeStruct((8, width), wide),
        ),
        in_specs=[VMEM_WHOLE] * 12,
        out_specs=(VMEM_WHOLE,) * 7,
        scratch_shapes=[
            pltpu.VMEM((rows, width), half),
            pltpu.VMEM((RING, rows, width), half),
            pltpu.VMEM((RING * rows, hidden), half),
            pltpu.VMEM((RING * rows, hidden), wide),
            pltpu.VMEM((rows, width), half),
            pltpu.VMEM((RING, rows, width), half),
            pltpu.VMEM((RING * rows, hidden), half),
            pltpu.SemaphoreType.DMA((4, Gather.slots)),
        ]
        + Scatter.scratch(width)
        + Scatter.scratch(width),
        compiler_params=pltpu.CompilerParams(
            collective_id=2, has_side_effects=True, vmem_limit_bytes=VMEM_BYTES
        ),
    )(attended, block_input, out_bias, gain1, bias1, up, up_bias, down, down_bias, gain2, bias2, cot)


def gather_kernel(x_ref, o_ref, send, recv):
    greet_ring()
    gather = Gather(x_ref, o_ref, send, recv)
    gather.start()
    for s in range(4):
        gather.ready(s)
    gather.finish()


def gather_rows(x):
    rows, width = x.shape
    out = pl.pallas_call(
        gather_kernel,
        out_shape=jax.ShapeDtypeStruct((RING, rows, width), x.dtype),
        in_specs=[VMEM_WHOLE],
        out_specs=VMEM_WHOLE,
        scratch_shapes=[pltpu.SemaphoreType.DMA((13,)), pltpu.SemaphoreType.DMA((13,))],
        compiler_params=pltpu.CompilerParams(collective_id=0, has_side_effects=True),
    )(x)
    return out.reshape(RING * rows, width)


def scatter_kernel(y_ref, o_ref, y, *scratch):
    greet_ring()
    scatter = Scatter(y_ref, *scratch)
    for k in (1, 3, 2, 0):
        scatter.computed(k)
    scatter.sides()
    scatter.across()
    scatter.through()
    o_ref[...] = scatter.result()
    scatter.finish()


def scatter_rows(y):
    tokens, width = y.shape
    rows = tokens // RING
    return pl.pallas_call(
        scatter_kernel,
        out_shape=jax.ShapeDtypeStruct((rows, width), wide),
        in_specs=[VMEM_WHOLE],
        out_specs=VMEM_WHOLE,
        scratch_shapes=Scatter.scratch(width),
        compiler_params=pltpu.CompilerParams(collective_id=1, has_side_effects=True),
    )(y.reshape(RING, rows, width))


class PlaneSum:
    def __init__(self, land, full, send, recv):
        self.land, self.full, self.send, self.recv = land, full, send, recv
        t, dp = lax.axis_index("tensor"), lax.axis_index("dp")
        self.t, self.dp = t, dp

    @staticmethod
    def peer(a, r):
        t, dp = lax.axis_index("tensor"), lax.axis_index("dp")
        other = lax.rem(dp // 4 + r // 4, 2) * 4 + lax.rem(dp + r, 4)
        return other, (other, lax.rem(t + a * RING, 2 * RING))

    @staticmethod
    def peers():
        return [PlaneSum.peer(n // PIECES, n % PIECES)[1] for n in range(1, 2 * PIECES)]

    def scatter(self, grads):
        for n in range(1, 2 * PIECES):
            piece, device = self.peer(n // PIECES, n % PIECES)
            remote(grads.at[n // PIECES, piece], self.land.at[n - 1], self.send, self.recv, n - 1, device).start()

    def share(self, grads):
        total = grads[0, self.dp].astype(wide)
        for n in range(15):
            place = self.land.at[n]
            remote(place, place, self.send, self.recv, n, (self.dp, self.t)).wait_recv()
            total += self.land[n].astype(wide)
        self.full[pl.ds(self.dp, 1)] = total.astype(half).reshape(1, *total.shape)
        for r in range(1, PIECES):
            place = self.full.at[self.dp]
            remote(place, place, self.send, self.recv, 14 + r, self.peer(0, r)[1]).start()

    def result(self, out):
        for r in range(1, PIECES):
            piece = lax.rem(self.dp // 4 + r // 4, 2) * 4 + lax.rem(self.dp + 8 - r, 4)
            place = self.full.at[piece]
            remote(place, place, self.send, self.recv, 14 + r, (self.dp, self.t)).wait_recv()
        out[...] = self.full[...].astype(wide)
        for n in range(22):
            place = self.land.at[0]
            remote(place, place, self.send, self.recv, n, (self.dp, self.t)).wait_send()

    @staticmethod
    def scratch(rows, width):
        return [
            pltpu.VMEM((15, rows, width), half),
            pltpu.VMEM((PIECES, rows, width), half),
            pltpu.SemaphoreType.DMA((22,)),
            pltpu.SemaphoreType.DMA((22,)),
        ]


class SmallSum:
    scratch = [
        pltpu.VMEM((8, 8, 1024), wide),
        pltpu.VMEM((2, 8, 1024), wide),
        pltpu.VMEM((15, 8, 1024), wide),
        pltpu.SemaphoreType.DMA((22,)),
        pltpu.SemaphoreType.DMA((22,)),
    ]

    def __init__(self, line, base, land, send, recv):
        self.line, self.base, self.land, self.send, self.recv = line, base, land, send, recv
        self.t, self.dp = lax.axis_index("tensor"), lax.axis_index("dp")

    @staticmethod
    def line_peer(r):
        t, dp = lax.axis_index("tensor"), lax.axis_index("dp")
        return (dp, (t // RING) * RING + lax.rem(t + r, RING))

    @staticmethod
    def peers():
        return [SmallSum.line_peer(r) for r in range(1, RING)]

    def start(self, vecs):
        for r in range(1, RING):
            remote(vecs, self.line.at[r], self.send, self.recv, 14 + r, self.line_peer(r)).start()

    def plane(self, vecs, shards):
        total = vecs[...]
        for r in range(1, RING):
            place = self.line.at[r]
            remote(place, place, self.send, self.recv, 14 + r, (self.dp, self.t)).wait_recv()
            total += self.line[r]
        row = lax.broadcasted_iota(jnp.int32, total.shape, 0)
        for a in range(2):
            self.base[a] = jnp.where(row == 6, jnp.broadcast_to(shards[pl.ds(a, 1)], total.shape), total)
        for n in range(1, 2 * PIECES):
            _, device = PlaneSum.peer(n // PIECES, n % PIECES)
            remote(self.base.at[n // PIECES], self.land.at[n - 1], self.send, self.recv, n - 1, device).start()

    def result(self):
        total = self.base[0]
        for n in range(15):
            place = self.land.at[n]
            remote(place, place, self.send, self.recv, n, (self.dp, self.t)).wait_recv()
            total += self.land[n]
        for n in range(22):
            place = self.land.at[0]
            remote(place, place, self.send, self.recv, n, (self.dp, self.t)).wait_send()
        return total


def reduce_kernel(count, *refs):
    grads, rest = refs[:count], refs[count:]
    vecs, shards, rest = rest[0], rest[1], rest[2:]
    outs, rest = rest[:count], rest[count:]
    small_out, rest = rest[0], rest[1:]
    small = SmallSum(*rest[:5])
    planes = [PlaneSum(*rest[5 + 4 * i : 9 + 4 * i]) for i in range(count)]
    greet(PlaneSum.peers() + SmallSum.peers())
    small.start(vecs)
    for plane, grad in zip(planes, grads):
        plane.scatter(grad)
    small.plane(vecs, shards)
    for plane, grad in zip(planes, grads):
        plane.share(grad)
    for plane, out in zip(planes, outs):
        plane.result(out)
    small_out[...] = small.result()


def reduce_all(grads, vecs, shards):
    scratch = list(SmallSum.scratch)
    for grad in grads:
        scratch += PlaneSum.scratch(*grad.shape[2:])
    return pl.pallas_call(
        functools.partial(reduce_kernel, len(grads)),
        out_shape=tuple(jax.ShapeDtypeStruct(grad.shape[1:], wide) for grad in grads)
        + (jax.ShapeDtypeStruct((8, 1024), wide),),
        in_specs=[VMEM_WHOLE] * (len(grads) + 2),
        out_specs=(VMEM_WHOLE,) * (len(grads) + 1),
        scratch_shapes=scratch,
        compiler_params=pltpu.CompilerParams(
            collective_id=3, has_side_effects=True, vmem_limit_bytes=VMEM_BYTES
        ),
    )(*grads, vecs, shards)


def masked_scores(queries, keys, segs):
    scores = jnp.einsum("qhd,khd->hqk", queries, keys, preferred_element_type=wide) * HEAD_DIM ** (-0.5)
    allowed = segs[:, None] == segs[None, :]
    return jnp.where(allowed[None], scores, MASKED)


def forward_seq(items):
    queries, keys, values, segs = items
    masked = masked_scores(queries, keys, segs)
    top = jnp.max(masked, axis=-1, keepdims=True)
    lse = top + jnp.log(jnp.sum(jnp.exp(masked - top), axis=-1, keepdims=True))
    probs = jnp.exp(masked - lse).astype(half)
    context = jnp.einsum("hqk,khd->qhd", probs, values, preferred_element_type=wide)
    return (context.astype(half), lse)


def backward_seq(items):
    queries, keys, values, segs, lse, d_context = items
    masked = masked_scores(queries, keys, segs)
    probs = jnp.exp(masked - lse)
    probs_half = probs.astype(half)
    d_values = jnp.einsum("hqk,qhd->khd", probs_half, d_context, preferred_element_type=wide)
    d_probs = jnp.einsum("qhd,khd->hqk", d_context, values, preferred_element_type=wide)
    d_scores = (
        probs * (d_probs - jnp.sum(probs * d_probs, axis=-1, keepdims=True)) * HEAD_DIM ** (-0.5)
    )
    d_scores = d_scores.astype(half)
    d_queries = jnp.einsum("hqk,khd->qhd", d_scores, keys, preferred_element_type=wide)
    d_keys = jnp.einsum("hqk,qhd->khd", d_scores, queries, preferred_element_type=wide)
    return (d_queries, d_keys, d_values)


def trade(arr):
    return lax.ppermute(arr, "tensor", [(t, (t + RING) % (2 * RING)) for t in range(2 * RING)])


def row(vector):
    return vector.reshape(1, vector.shape[0])


def per_device(
    block_input,
    segment_ids,
    qkv_weight,
    qv_bias,
    out_weight,
    out_bias,
    norm1_gain,
    norm1_bias,
    up_weight,
    up_bias,
    down_weight,
    down_bias,
    norm2_gain,
    norm2_bias,
    cotangent,
):
    my_seq = lax.axis_index("tensor") // RING
    segs = lax.dynamic_index_in_dim(segment_ids, my_seq, 0, keepdims=False)
    seq_len = segs.shape[0]
    qkv_rows = jnp.swapaxes(qkv_weight, 1, 2)
    qkv_two = jnp.concatenate([qkv_rows, trade(qkv_rows)], axis=1)
    qv_bias_two = jnp.concatenate([qv_bias, trade(qv_bias)], axis=1)
    out_two = jnp.concatenate([out_weight, trade(out_weight)], axis=0)
    up_two = jnp.concatenate([up_weight, trade(up_weight)], axis=1)
    up_bias_two = jnp.concatenate([up_bias, trade(up_bias)], axis=0)
    down_two = jnp.concatenate([down_weight, trade(down_weight)], axis=0)

    gathered = gather_rows(block_input)
    projected = jnp.einsum("td,cwd->ctw", gathered, qkv_two, preferred_element_type=wide)
    queries = (projected[0] + qv_bias_two[0]).astype(half)
    keys = projected[1].astype(half)
    values = (projected[2] + qv_bias_two[1]).astype(half)
    width = queries.shape[1]

    def by_head(arr):
        return arr.reshape(seq_len, width // HEAD_DIM, HEAD_DIM)

    context, lse = forward_seq((by_head(queries), by_head(keys), by_head(values), segs))
    context = context.reshape(seq_len, width)
    attended = scatter_rows(jnp.dot(context, out_two, preferred_element_type=wide).astype(half))

    output, d_first, d_first_half, g_up, g_down, g_up_bias, vecs = feed_forward(
        attended, block_input, row(out_bias), row(norm1_gain), row(norm1_bias), up_two, row(up_bias_two),
        down_two, row(down_bias), row(norm2_gain), row(norm2_bias), cotangent,
    )

    d_first_all = gather_rows(d_first_half)
    g_out = jnp.einsum("tw,td->wd", context, d_first_all, preferred_element_type=wide)
    d_context = jnp.einsum("td,wd->tw", d_first_all, out_two, preferred_element_type=wide).astype(half)
    d_queries, d_keys, d_values = (
        arr.reshape(seq_len, width)
        for arr in backward_seq(
            (by_head(queries), by_head(keys), by_head(values), segs, lse, by_head(d_context))
        )
    )
    g_qv_bias = jnp.concatenate(
        [arr.reshape(2, HEAD_DIM) for arr in (jnp.sum(d_queries, axis=0), jnp.sum(d_values, axis=0))], axis=1
    )
    d_qkv = jnp.stack([d_queries, d_keys, d_values]).astype(half)
    g_qkv = jnp.einsum("ctw,td->cwd", d_qkv, gathered, preferred_element_type=wide)
    d_rows = jnp.einsum("ctw,cwd->td", d_qkv, qkv_two, preferred_element_type=wide)
    input_grad = (d_first + scatter_rows(d_rows.astype(half))).astype(half)

    pieces = g_up.reshape(2, PIECES, g_up.shape[1] // PIECES, g_up.shape[2])
    down_pieces = g_down.reshape(2, PIECES, g_down.shape[1] // PIECES, g_down.shape[2])
    g_qkv = g_qkv.astype(half).reshape(3, 2, HEAD_DIM, -1)
    g_out = g_out.astype(half).reshape(1, 2, HEAD_DIM, -1)
    late = jnp.swapaxes(jnp.concatenate([g_qkv, g_out], axis=0), 0, 1)
    late = late.reshape(2, PIECES, 4 * HEAD_DIM // PIECES, -1)
    shards = jnp.concatenate(
        [g_up_bias.reshape(2, -1), g_qv_bias, jnp.zeros((2, 1024 - g_up_bias.shape[1] // 2 - 2 * HEAD_DIM), wide)],
        axis=1,
    )
    up_sum, down_sum, late_sum, small = reduce_all((pieces, down_pieces, late), vecs, shards)
    ff = up_bias.shape[0]
    late_sum = late_sum.reshape(4, HEAD_DIM, -1)
    return (
        output,
        input_grad,
        jnp.swapaxes(late_sum[:3], 1, 2),
        small[6, ff : ff + 2 * HEAD_DIM].reshape(2, HEAD_DIM),
        late_sum[3],
        small[0],
        small[1],
        small[2],
        up_sum.reshape(up_weight.shape),
        small[6, :ff],
        down_sum.reshape(down_weight.shape),
        small[3],
        small[4],
        small[5],
    )


def solution(mesh):
    placed = (
        P(("dp", "tensor"), None),
        P("dp", None),
        P(None, None, "tensor"),
        P(None, "tensor"),
        P("tensor", None),
        P(),
        P(),
        P(),
        P(None, "tensor"),
        P("tensor"),
        P("tensor", None),
        P(),
        P(),
        P(),
        P(("dp", "tensor"), None),
    )
    return jax.shard_map(
        per_device,
        mesh=mesh,
        in_specs=placed,
        out_specs=(
            P(("dp", "tensor"), None),
            P(("dp", "tensor"), None),
            P(None, None, "tensor"),
            P(None, "tensor"),
            P("tensor", None),
            P(),
            P(),
            P(),
            P(None, "tensor"),
            P("tensor"),
            P("tensor", None),
            P(),
            P(),
            P(),
        ),
        check_vma=False,
    )
```

```python
import jax
import jax.numpy as jnp
from jax import lax
from jax.experimental import pallas as pl
from jax.experimental.pallas import tpu as pltpu
from jax.sharding import PartitionSpec as P

HEAD_DIM = 64
RING = 8
BLOCK = 128
HALF = 64
CHIP = 2 * BLOCK
PIECES = 8
MESH = pl.DeviceIdType.MESH
VMEM_WHOLE = pl.BlockSpec(memory_space=pltpu.VMEM)
VMEM_BYTES = 60 * 1024 * 1024
half = jnp.bfloat16
wide = jnp.float32


EPS = 1e-12
MASKED = -1e30
ROOT_HALF = 0.7071067811865476
INV_ROOT_TAU = 0.3989422804014327


def ring_place():
    t = lax.axis_index("tensor")
    dp = lax.axis_index("dp")
    base = (t // RING) * RING
    j = t % RING
    x = j // 2
    c = j % 2

    def block_of(step, other=False):
        xx = lax.rem(x + step + 4, 4)
        return xx * 2 + ((1 - c) if other else c)

    def device_of(step, other=False):
        return (dp, base + block_of(step, other))

    return block_of, device_of


def ring_order(s):
    return s + s // 2 - 2 * (s // 3)


def greet(devices):
    barrier = pltpu.get_barrier_semaphore()
    for device in devices:
        pl.semaphore_signal(barrier, inc=1, device_id=device, device_id_type=MESH)
    pl.semaphore_wait(barrier, len(devices))


def greet_ring():
    _, device_of = ring_place()
    greet((device_of(1), device_of(-1), device_of(0, True)))


def remote(src, dst, send, recv, slot, device):
    return pltpu.make_async_remote_copy(
        src_ref=src,
        dst_ref=dst,
        send_sem=send.at[slot],
        recv_sem=recv.at[slot],
        device_id=device,
        device_id_type=MESH,
    )


FIRST = pl.ds(0, HALF)
SECOND = pl.ds(HALF, HALF)


class Gather:
    slots = 13

    def __init__(self, src, out, send, recv):
        self.src, self.out, self.send, self.recv = src, out, send, recv
        self.block_of, self.device_of = ring_place()
        self.partner = self.device_of(0, True)

    def copy(self, place, slot, device):
        return remote(place, place, self.send, self.recv, slot, device)

    def start(self):
        src, at = self.src, self.out.at
        mine, right, left = self.block_of(0), self.device_of(1), self.device_of(-1)
        for part, slot, device in ((FIRST, 0, right), (SECOND, 3, left), (SECOND, 1, right), (FIRST, 2, left)):
            remote(src.at[part], at[mine, part], self.send, self.recv, slot, device).start()
        remote(src, at[mine], self.send, self.recv, 6, self.partner).start()
        self.out[pl.ds(mine, 1)] = src[...].reshape(1, *src.shape)

    def pass_on(self, slot, step, part, share_slot, device=None, device_slot=None):
        place = self.out.at[self.block_of(step), part]
        self.copy(place, slot, self.partner).wait_recv()
        if device is not None:
            self.copy(place, device_slot, device).start()
        self.copy(place, share_slot, self.partner).start()

    def shared(self, step, slots):
        for slot, part in zip(slots, (FIRST, SECOND)):
            self.copy(self.out.at[self.block_of(step, True), part], slot, self.partner).wait_recv()

    def ready(self, s):
        @pl.when(s == 0)
        def _():
            self.copy(self.out.at[self.block_of(0, True)], 6, self.partner).wait_recv()

        @pl.when(s == 1)
        def _():
            self.pass_on(0, -1, FIRST, 7, self.device_of(1), 4)
            self.pass_on(3, 1, SECOND, 10, self.device_of(-1), 5)
            self.pass_on(2, 1, FIRST, 9)
            self.pass_on(1, -1, SECOND, 8)
            self.shared(1, (9, 10))

        @pl.when(s == 2)
        def _():
            self.shared(-1, (7, 8))

        @pl.when(s == 3)
        def _():
            self.pass_on(4, 2, FIRST, 11)
            self.pass_on(5, 2, SECOND, 12)
            self.shared(2, (11, 12))

    def finish(self):
        half_place = self.out.at[0, FIRST]
        for slot in range(13):
            self.copy(self.out.at[0] if slot == 6 else half_place, slot, self.partner).wait_send()


class Scatter:
    slots = 10

    @staticmethod
    def scratch(width):
        return [
            pltpu.VMEM((RING, BLOCK, width), half),
            pltpu.VMEM((4, BLOCK, width), half),
            pltpu.VMEM((6, HALF, width), half),
            pltpu.VMEM((2, HALF, width), half),
            pltpu.VMEM((2, 2, HALF, width), half),
            pltpu.SemaphoreType.DMA((10,)),
            pltpu.SemaphoreType.DMA((10,)),
        ]

    def __init__(self, y, pair, stage, transit, final, send, recv):
        self.y, self.pair, self.stage, self.transit, self.final = y, pair, stage, transit, final
        self.send, self.recv = send, recv
        self.block_of, self.device_of = ring_place()
        self.partner = self.device_of(0, True)

    def computed(self, k):
        remote(self.y.at[self.block_of(k, True)], self.pair.at[k], self.send, self.recv, k, self.partner).start()

    def arrived(self, place, slot):
        remote(place, place, self.send, self.recv, slot, self.partner).wait_recv()

    def chip_sum(self, k, part):
        return self.y[self.block_of(k), part].astype(wide) + self.pair[k, part].astype(wide)

    def forward(self, at, value, place, slot, device):
        self.stage[at] = value.astype(half)
        remote(self.stage.at[at], place, self.send, self.recv, slot, device).start()

    def sides(self):
        self.arrived(self.pair.at[1], 1)
        self.forward(2, self.chip_sum(1, SECOND), self.final.at[0, 1], 6, self.device_of(1))
        self.arrived(self.pair.at[3], 3)
        self.forward(3, self.chip_sum(3, FIRST), self.final.at[1, 0], 7, self.device_of(-1))

    def across(self):
        self.arrived(self.pair.at[2], 2)
        self.forward(0, self.chip_sum(2, FIRST), self.transit.at[0], 4, self.device_of(1))
        self.forward(1, self.chip_sum(2, SECOND), self.transit.at[1], 5, self.device_of(-1))

    def through(self):
        self.arrived(self.transit.at[0], 4)
        value = self.chip_sum(1, FIRST) + self.transit[0].astype(wide)
        self.forward(4, value, self.final.at[0, 0], 8, self.device_of(1))
        self.arrived(self.transit.at[1], 5)
        value = self.chip_sum(3, SECOND) + self.transit[1].astype(wide)
        self.forward(5, value, self.final.at[1, 1], 9, self.device_of(-1))

    def result(self):
        self.arrived(self.pair.at[0], 0)
        for slot, place in ((6, (0, 1)), (7, (1, 0)), (8, (0, 0)), (9, (1, 1))):
            self.arrived(self.final.at[place], slot)
        final = self.final
        rows = [
            self.chip_sum(0, part) + final[0, h].astype(wide) + final[1, h].astype(wide)
            for h, part in enumerate((FIRST, SECOND))
        ]
        return jnp.concatenate(rows, axis=0)

    def finish(self):
        for slot in range(10):
            place = self.pair.at[0] if slot < 4 else self.transit.at[0]
            remote(place, place, self.send, self.recv, slot, self.partner).wait_send()


def dot_nn(left, right):
    return lax.dot_general(left, right, (((1,), (0,)), ((), ())), preferred_element_type=wide)


def dot_nt(left, right):
    return lax.dot_general(left, right, (((1,), (1,)), ((), ())), preferred_element_type=wide)


def dot_tn(left, right):
    return lax.dot_general(left, right, (((0,), (0,)), ((), ())), preferred_element_type=wide)


def layer_norm(rows, gain, shift):
    center = rows - jnp.mean(rows, axis=-1, keepdims=True)
    inverse = lax.rsqrt(jnp.mean(center * center, axis=-1, keepdims=True) + EPS)
    normed = center * inverse
    return (normed * gain + shift, normed, inverse)


def norm_back(grad, normed, inverse, gain):
    scaled = grad * gain
    return inverse * (
        scaled
        - jnp.mean(scaled, axis=-1, keepdims=True)
        - normed * jnp.mean(scaled * normed, axis=-1, keepdims=True)
    )


def gelu_parts(pre):
    cumul = 0.5 * (1.0 + lax.erf(pre * ROOT_HALF))
    return (pre * cumul, cumul + pre * jnp.exp(-0.5 * pre * pre) * INV_ROOT_TAU)


def column_sum(rows):
    return jnp.sum(rows, axis=0, keepdims=True)


def chip_rows(ref, chip):
    block = ref[pl.ds(2 * chip, 2)]
    return block.reshape(CHIP, block.shape[2])


def flat_rows(ref):
    block = ref[...]
    return block.reshape(block.shape[0] * block.shape[1], block.shape[2])


def feed_forward_kernel(
    attended, block_input, out_bias, gain1, bias1, up, bias_two, down, down_bias, gain2, bias2, cot,
    out, d_first, d_first_half, g_up, g_down, g_up_bias, vecs,
    hidden_half, hidden_all, act, slope, d_second_half, d_second_all, d_pre, gather_sems, *scatter_scratch,
):
    block_of, _ = ring_place()
    shard = up.shape[2]
    greet_ring()
    first = block_input[...].astype(wide) + attended[...] + out_bias[...]
    hidden, normed_one, inverse_one = layer_norm(first, gain1[...], bias1[...])
    hidden_half[...] = hidden.astype(half)
    gather = Gather(hidden_half, hidden_all, gather_sems.at[0], gather_sems.at[1])
    scatter = Scatter(*scatter_scratch[:7])
    gather.start()

    @pl.loop(0, 4)
    def _(s):
        gather.ready(s)
        k = ring_order(s)
        chip = block_of(k) // 2
        rows = pl.ds(chip * CHIP, CHIP)
        for a in range(2):
            pre = dot_nn(chip_rows(hidden_all, chip), up[a]) + bias_two[a, :, :shard]
            value, gelu_slope = gelu_parts(pre)
            act[rows, a * shard : (a + 1) * shard] = value.astype(half)
            slope[rows, a * shard : (a + 1) * shard] = gelu_slope
        term = dot_nn(act[rows], flat_rows(down)).astype(half)
        scatter.y[pl.ds(2 * chip, 2)] = term.reshape(2, BLOCK, term.shape[1])
        scatter.computed(k)

    scatter.sides()
    scatter.across()
    gather.finish()
    scatter.through()
    second = hidden + scatter.result() + down_bias[...]
    scatter.finish()
    output, normed_two, inverse_two = layer_norm(second, gain2[...], bias2[...])
    out[...] = output.astype(half)
    grad = cot[...].astype(wide)
    d_second = norm_back(grad, normed_two, inverse_two, gain2[...])
    d_second_half[...] = d_second.astype(half)
    gather = Gather(d_second_half, d_second_all, gather_sems.at[2], gather_sems.at[3])
    scatter = Scatter(*scatter_scratch[7:])
    gather.start()
    vecs[pl.ds(3, 1)] = column_sum(d_second)
    vecs[pl.ds(4, 1)] = column_sum(grad * normed_two)
    vecs[pl.ds(5, 1)] = column_sum(grad)
    vecs[pl.ds(6, 2)] = jnp.zeros((2, grad.shape[1]), wide)
    g_up_bias[...] = jnp.zeros_like(g_up_bias)

    @pl.loop(0, 4)
    def _(s):
        gather.ready(s)
        k = ring_order(s)
        chip = block_of(k) // 2
        rows = pl.ds(chip * CHIP, CHIP)
        grad_pre = dot_nt(chip_rows(d_second_all, chip), flat_rows(down)) * slope[rows]
        g_up_bias[...] += column_sum(grad_pre)
        grad_pre = grad_pre.astype(half)
        d_pre[rows] = grad_pre
        term = dot_nt(grad_pre[:, :shard], up[0]) + dot_nt(grad_pre[:, shard:], up[1])
        term = term.astype(half)
        scatter.y[pl.ds(2 * chip, 2)] = term.reshape(2, BLOCK, term.shape[1])
        scatter.computed(k)

    scatter.sides()
    scatter.across()
    gather.finish()
    for a in range(2):
        part = dot_tn(act[:, a * shard : (a + 1) * shard], flat_rows(d_second_all)).astype(half)
        g_down[a] = part.reshape(PIECES, shard // PIECES, part.shape[1])
    scatter.through()

    @pl.loop(0, 4)
    def _(i):
        columns = pl.ds(pl.multiple_of(i * 256, 256), 256)
        left = hidden_all[:, :, columns].reshape(RING * BLOCK, 256)
        part = dot_tn(left, d_pre[...]).astype(half)
        for a in range(2):
            g_up[a, pl.ds(2 * i, 2)] = part[:, a * shard : (a + 1) * shard].reshape(2, BLOCK, shard)

    d_hidden = d_second + scatter.result()
    scatter.finish()
    grad_first = norm_back(d_hidden, normed_one, inverse_one, gain1[...])
    d_first[...] = grad_first
    d_first_half[...] = grad_first.astype(half)
    vecs[pl.ds(0, 1)] = column_sum(grad_first)
    vecs[pl.ds(1, 1)] = column_sum(d_hidden * normed_one)
    vecs[pl.ds(2, 1)] = column_sum(d_hidden)


def feed_forward(attended, block_input, out_bias, gain1, bias1, up, bias_two, down, down_bias, gain2, bias2, cot):
    rows, width = attended.shape
    shard = up.shape[2]
    hidden = 2 * shard
    return pl.pallas_call(
        feed_forward_kernel,
        out_shape=(
            jax.ShapeDtypeStruct((rows, width), half),
            jax.ShapeDtypeStruct((rows, width), wide),
            jax.ShapeDtypeStruct((rows, width), half),
            jax.ShapeDtypeStruct((2, PIECES, width // PIECES, shard), half),
            jax.ShapeDtypeStruct((2, PIECES, shard // PIECES, width), half),
            jax.ShapeDtypeStruct((1, hidden), wide),
            jax.ShapeDtypeStruct((8, width), wide),
        ),
        in_specs=[VMEM_WHOLE] * 12,
        out_specs=(VMEM_WHOLE,) * 7,
        scratch_shapes=[
            pltpu.VMEM((rows, width), half),
            pltpu.VMEM((RING, rows, width), half),
            pltpu.VMEM((RING * rows, hidden), half),
            pltpu.VMEM((RING * rows, hidden), wide),
            pltpu.VMEM((rows, width), half),
            pltpu.VMEM((RING, rows, width), half),
            pltpu.VMEM((RING * rows, hidden), half),
            pltpu.SemaphoreType.DMA((4, Gather.slots)),
        ]
        + Scatter.scratch(width)
        + Scatter.scratch(width),
        compiler_params=pltpu.CompilerParams(
            collective_id=2, has_side_effects=True, vmem_limit_bytes=VMEM_BYTES
        ),
    )(attended, block_input, out_bias, gain1, bias1, up, bias_two, down, down_bias, gain2, bias2, cot)


class PlaneSum:
    def __init__(self, land, full, send, recv):
        self.land, self.full, self.send, self.recv = land, full, send, recv
        t, dp = lax.axis_index("tensor"), lax.axis_index("dp")
        self.t, self.dp = t, dp

    @staticmethod
    def peer(a, r):
        t, dp = lax.axis_index("tensor"), lax.axis_index("dp")
        other = lax.rem(dp // 4 + r // 4, 2) * 4 + lax.rem(dp + r, 4)
        return other, (other, lax.rem(t + a * RING, 2 * RING))

    @staticmethod
    def peers():
        return [PlaneSum.peer(n // PIECES, n % PIECES)[1] for n in range(1, 2 * PIECES)]

    def scatter(self, grads):
        for n in range(1, 2 * PIECES):
            piece, device = self.peer(n // PIECES, n % PIECES)
            remote(grads.at[n // PIECES, piece], self.land.at[n - 1], self.send, self.recv, n - 1, device).start()

    def share(self, grads):
        total = grads[0, self.dp].astype(wide)
        for n in range(15):
            place = self.land.at[n]
            remote(place, place, self.send, self.recv, n, (self.dp, self.t)).wait_recv()
            total += self.land[n].astype(wide)
        self.full[pl.ds(self.dp, 1)] = total.astype(half).reshape(1, *total.shape)
        for r in range(1, PIECES):
            place = self.full.at[self.dp]
            remote(place, place, self.send, self.recv, 14 + r, self.peer(0, r)[1]).start()

    def result(self, out):
        for r in range(1, PIECES):
            piece = lax.rem(self.dp // 4 + r // 4, 2) * 4 + lax.rem(self.dp + 8 - r, 4)
            place = self.full.at[piece]
            remote(place, place, self.send, self.recv, 14 + r, (self.dp, self.t)).wait_recv()
        out[...] = self.full[...].astype(wide)
        for n in range(22):
            place = self.land.at[0]
            remote(place, place, self.send, self.recv, n, (self.dp, self.t)).wait_send()

    @staticmethod
    def scratch(rows, width):
        return [
            pltpu.VMEM((15, rows, width), half),
            pltpu.VMEM((PIECES, rows, width), half),
            pltpu.SemaphoreType.DMA((22,)),
            pltpu.SemaphoreType.DMA((22,)),
        ]


class SmallSum:
    scratch = [
        pltpu.VMEM((8, 8, 1024), wide),
        pltpu.VMEM((2, 8, 1024), wide),
        pltpu.VMEM((15, 8, 1024), wide),
        pltpu.SemaphoreType.DMA((22,)),
        pltpu.SemaphoreType.DMA((22,)),
    ]

    def __init__(self, line, base, land, send, recv):
        self.line, self.base, self.land, self.send, self.recv = line, base, land, send, recv
        self.t, self.dp = lax.axis_index("tensor"), lax.axis_index("dp")

    @staticmethod
    def line_peer(r):
        t, dp = lax.axis_index("tensor"), lax.axis_index("dp")
        return (dp, (t // RING) * RING + lax.rem(t + r, RING))

    @staticmethod
    def peers():
        return [SmallSum.line_peer(r) for r in range(1, RING)]

    def start(self, vecs):
        for r in range(1, RING):
            remote(vecs, self.line.at[r], self.send, self.recv, 14 + r, self.line_peer(r)).start()

    def plane(self, vecs, shard_rows):
        total = vecs[...]
        for r in range(1, RING):
            place = self.line.at[r]
            remote(place, place, self.send, self.recv, 14 + r, (self.dp, self.t)).wait_recv()
            total += self.line[r]
        row = lax.broadcasted_iota(jnp.int32, total.shape, 0)
        for a in range(2):
            self.base[a] = jnp.where(row == 6, jnp.broadcast_to(shard_rows[a], total.shape), total)
        for n in range(1, 2 * PIECES):
            _, device = PlaneSum.peer(n // PIECES, n % PIECES)
            remote(self.base.at[n // PIECES], self.land.at[n - 1], self.send, self.recv, n - 1, device).start()

    def result(self):
        total = self.base[0]
        for n in range(15):
            place = self.land.at[n]
            remote(place, place, self.send, self.recv, n, (self.dp, self.t)).wait_recv()
            total += self.land[n]
        for n in range(22):
            place = self.land.at[0]
            remote(place, place, self.send, self.recv, n, (self.dp, self.t)).wait_send()
        return total


def pair_of(shape):
    return jax.ShapeDtypeStruct((2, *shape.shape), shape.dtype)


def segment_column(ids, column):
    upper = lax.axis_index("tensor") // RING
    numbers = jnp.where(upper == 0, ids[pl.ds(0, 1)], ids[pl.ds(1, 1)])
    column[...] = jnp.transpose(jnp.broadcast_to(numbers, (128, numbers.shape[1])))
    return numbers


def attention_kernel(
    x, ids, qkv, out_weight, up, down, bias,
    attended, x_all, queries, keys, values, lse, context, qkv_two, out_two, up_two, down_two, bias_two,
    column, gather_sems, trade_sems, *scatter_scratch,
):
    block_of, device_of = ring_place()
    across_z = (lax.axis_index("dp"), lax.rem(lax.axis_index("tensor") + RING, 2 * RING))
    greet((device_of(1), device_of(-1), device_of(0, True), across_z))
    gather = Gather(x, x_all, gather_sems.at[0], gather_sems.at[1])
    scatter = Scatter(*scatter_scratch)
    gather.start()
    pairs = ((bias, bias_two), (qkv, qkv_two), (out_weight, out_two), (up, up_two), (down, down_two))
    trades = [
        remote(mine, two.at[1], trade_sems.at[0], trade_sems.at[1], slot, across_z)
        for slot, (mine, two) in enumerate(pairs)
    ]
    for trade in trades:
        trade.start()
    for mine, two in pairs:
        two[0] = mine[...]
    numbers = segment_column(ids, column)
    ff = up.shape[1]

    def project(a, chip):
        rows = pl.ds(chip * CHIP, CHIP)
        product = dot_nt(chip_rows(x_all, chip), qkv_two[a].reshape(3 * HEAD_DIM, x.shape[1]))
        parts = [product[:, i * HEAD_DIM : (i + 1) * HEAD_DIM] for i in range(3)]
        queries[a, rows] = (parts[0] + bias_two[a, :, ff : ff + HEAD_DIM]).astype(half)
        keys[a, rows] = parts[1].astype(half)
        values[a, rows] = (parts[2] + bias_two[a, :, ff + HEAD_DIM : ff + 2 * HEAD_DIM]).astype(half)

    @pl.loop(0, 4)
    def _(s):
        gather.ready(s)
        project(0, block_of(ring_order(s)) // 2)

    trades[0].wait_recv()
    trades[1].wait_recv()

    @pl.loop(0, 4)
    def _(chip):
        project(1, chip)

    trades[2].wait_recv()

    @pl.loop(0, 4)
    def _(i):
        k = ring_order(3 - i)
        chip = block_of(k) // 2
        rows = pl.ds(chip * CHIP, CHIP)
        allowed = column[rows, 0:1] == numbers
        for a in range(2):
            scores = dot_nt(queries[a, rows] * HEAD_DIM ** (-0.5), keys[a])
            masked = jnp.where(allowed, scores, MASKED)
            top = jnp.max(masked, axis=-1, keepdims=True)
            weights = jnp.exp(masked - top)
            mass = jnp.sum(weights, axis=-1, keepdims=True)
            lse[a, rows] = top + jnp.log(mass)
            probs = (weights * (1.0 / mass)).astype(half)
            context[rows, a * HEAD_DIM : (a + 1) * HEAD_DIM] = dot_nn(probs, values[a]).astype(half)
        term = dot_nn(context[rows], flat_rows(out_two)).astype(half)
        scatter.y[pl.ds(2 * chip, 2)] = term.reshape(2, BLOCK, term.shape[1])
        scatter.computed(k)

        @pl.when(i == 1)
        def _():
            scatter.across()

    scatter.sides()
    gather.finish()
    scatter.through()
    attended[...] = scatter.result()
    scatter.finish()
    trades[3].wait_recv()
    trades[4].wait_recv()
    for trade in trades:
        trade.wait_send()


def attention(x, ids, qkv, out_weight, up, down, bias):
    rows, width = x.shape
    tokens = RING * rows
    head = jax.ShapeDtypeStruct((2, tokens, HEAD_DIM), half)
    return pl.pallas_call(
        attention_kernel,
        out_shape=(
            jax.ShapeDtypeStruct((rows, width), wide),
            jax.ShapeDtypeStruct((RING, rows, width), half),
            head,
            head,
            head,
            jax.ShapeDtypeStruct((2, tokens, 1), wide),
            jax.ShapeDtypeStruct((tokens, 2 * HEAD_DIM), half),
            pair_of(qkv),
            pair_of(out_weight),
            pair_of(up),
            pair_of(down),
            pair_of(bias),
        ),
        in_specs=[VMEM_WHOLE] * 7,
        out_specs=(VMEM_WHOLE,) * 12,
        scratch_shapes=[
            pltpu.VMEM((tokens, 128), jnp.int32),
            pltpu.SemaphoreType.DMA((2, Gather.slots)),
            pltpu.SemaphoreType.DMA((2, 5)),
        ]
        + Scatter.scratch(width),
        compiler_params=pltpu.CompilerParams(
            collective_id=0, has_side_effects=True, vmem_limit_bytes=VMEM_BYTES
        ),
    )(x, ids, qkv, out_weight, up, down, bias)


def attention_back_kernel(
    d_first, d_first_half, x_all, ids, queries, keys, values, lse, context, qkv_two, out_two,
    g_up, g_down, g_up_bias, vecs,
    input_grad, up_sum, down_sum, late_sum, small_out,
    d_first_all, column, d_keys, d_values, d_qkv, query_sum, late, gather_sems, *scratch,
):
    block_of, _ = ring_place()
    scatter, scratch = Scatter(*scratch[:7]), scratch[7:]
    small, scratch = SmallSum(*scratch[:5]), scratch[5:]
    early = [(PlaneSum(*scratch[:4]), g_up, up_sum), (PlaneSum(*scratch[4:8]), g_down, down_sum)]
    last = PlaneSum(*scratch[8:])
    greet(PlaneSum.peers() + SmallSum.peers())
    gather = Gather(d_first_half, d_first_all, gather_sems.at[0], gather_sems.at[1])
    gather.start()
    small.start(vecs)
    for plane, grads, _ in early:
        plane.scatter(grads)
    numbers = segment_column(ids, column)
    d_keys[...] = jnp.zeros_like(d_keys)
    d_values[...] = jnp.zeros_like(d_values)
    query_sum[...] = jnp.zeros_like(query_sum)
    group = 3 * HEAD_DIM

    @pl.loop(0, 4)
    def _(s):
        gather.ready(s)
        chip = block_of(ring_order(s)) // 2
        rows = pl.ds(chip * CHIP, CHIP)
        d_context = dot_nt(chip_rows(d_first_all, chip), flat_rows(out_two)).astype(half)
        allowed = column[rows, 0:1] == numbers
        for a in range(2):
            d_head = d_context[:, a * HEAD_DIM : (a + 1) * HEAD_DIM]
            query = queries[a, rows]
            scores = dot_nt(query * HEAD_DIM ** (-0.5), keys[a])
            probs = jnp.exp(jnp.where(allowed, scores, MASKED) - lse[a, rows])
            d_values[a] += dot_tn(d_head, probs.astype(half))
            d_probs = dot_nt(d_head * HEAD_DIM ** (-0.5), values[a])
            mean = jnp.sum(probs * d_probs, axis=-1, keepdims=True)
            d_scores = (probs * (d_probs - mean)).astype(half)
            d_query = dot_nn(d_scores, keys[a])
            query_sum[a] += column_sum(d_query)
            d_qkv[rows, a * group : a * group + HEAD_DIM] = d_query.astype(half)
            d_keys[a] += dot_tn(query, d_scores)

    gather.finish()
    shard_rows = []
    shard = g_up_bias.shape[1] // 2
    for a in range(2):
        at = a * group + HEAD_DIM
        d_qkv[:, at : at + HEAD_DIM] = jnp.transpose(d_keys[a].astype(half))
        d_qkv[:, at + HEAD_DIM : at + 2 * HEAD_DIM] = jnp.transpose(d_values[a].astype(half))
        value_sum = jnp.sum(d_values[a], axis=1, keepdims=True)
        value_sum = jnp.transpose(jnp.broadcast_to(value_sum, (HEAD_DIM, 128)))[0:1]
        shard_rows.append(
            jnp.concatenate(
                [
                    g_up_bias[:, a * shard : (a + 1) * shard],
                    query_sum[a],
                    value_sum,
                    jnp.zeros((1, vecs.shape[1] - shard - 2 * HEAD_DIM), wide),
                ],
                axis=1,
            )
        )
    grad_out = dot_tn(context[...], flat_rows(d_first_all)).astype(half)
    piece = late.shape[2]
    for a in range(2):
        part = dot_tn(d_qkv[:, a * group : (a + 1) * group], flat_rows(x_all)).astype(half)
        late[a, pl.ds(0, 6)] = part.reshape(6, piece, part.shape[1])
        part = grad_out[a * HEAD_DIM : (a + 1) * HEAD_DIM]
        late[a, pl.ds(6, 2)] = part.reshape(2, piece, part.shape[1])
    last.scatter(late)
    small.plane(vecs, shard_rows)

    @pl.loop(0, 4)
    def _(i):
        k = ring_order(3 - i)
        chip = block_of(k) // 2
        weight = qkv_two[...].reshape(2 * group, d_first.shape[1])
        term = dot_nn(d_qkv[pl.ds(chip * CHIP, CHIP)], weight).astype(half)
        scatter.y[pl.ds(2 * chip, 2)] = term.reshape(2, BLOCK, term.shape[1])
        scatter.computed(k)

        @pl.when(i == 1)
        def _():
            scatter.across()

    scatter.sides()
    scatter.through()
    for plane, grads, _ in early:
        plane.share(grads)
    input_grad[...] = (d_first[...] + scatter.result()).astype(half)
    scatter.finish()
    last.share(late)
    for plane, _, total in early:
        plane.result(total)
    last.result(late_sum)
    small_out[...] = small.result()


def attention_back(d_first, d_first_half, x_all, ids, heads, lse, context, qkv_two, out_two, g_up, g_down, g_up_bias, vecs):
    rows, width = d_first.shape
    tokens = RING * rows
    late = (PIECES, 4 * HEAD_DIM // PIECES, width)
    return pl.pallas_call(
        attention_back_kernel,
        out_shape=(
            jax.ShapeDtypeStruct((rows, width), half),
            jax.ShapeDtypeStruct(g_up.shape[1:], wide),
            jax.ShapeDtypeStruct(g_down.shape[1:], wide),
            jax.ShapeDtypeStruct(late, wide),
            jax.ShapeDtypeStruct(vecs.shape, wide),
        ),
        in_specs=[VMEM_WHOLE] * 15,
        out_specs=(VMEM_WHOLE,) * 5,
        scratch_shapes=[
            pltpu.VMEM((RING, rows, width), half),
            pltpu.VMEM((tokens, 128), jnp.int32),
            pltpu.VMEM((2, HEAD_DIM, tokens), wide),
            pltpu.VMEM((2, HEAD_DIM, tokens), wide),
            pltpu.VMEM((tokens, 6 * HEAD_DIM), half),
            pltpu.VMEM((2, 1, HEAD_DIM), wide),
            pltpu.VMEM((2, *late), half),
            pltpu.SemaphoreType.DMA((2, Gather.slots)),
        ]
        + Scatter.scratch(width)
        + SmallSum.scratch
        + PlaneSum.scratch(*g_up.shape[2:])
        + PlaneSum.scratch(*g_down.shape[2:])
        + PlaneSum.scratch(*late[1:]),
        compiler_params=pltpu.CompilerParams(
            collective_id=1, has_side_effects=True, vmem_limit_bytes=VMEM_BYTES
        ),
    )(d_first, d_first_half, x_all, ids, *heads, lse, context, qkv_two, out_two, g_up, g_down, g_up_bias, vecs)


def row(vector):
    return vector.reshape(1, vector.shape[0])


def per_device(
    block_input,
    segment_ids,
    qkv_weight,
    qv_bias,
    out_weight,
    out_bias,
    norm1_gain,
    norm1_bias,
    up_weight,
    up_bias,
    down_weight,
    down_bias,
    norm2_gain,
    norm2_bias,
    cotangent,
):
    bias = row(jnp.concatenate([up_bias, qv_bias.reshape(-1)]))
    attended, x_all, queries, keys, values, lse, context, qkv_two, out_two, up_two, down_two, bias_two = attention(
        block_input, segment_ids, jnp.swapaxes(qkv_weight, 1, 2), out_weight, up_weight, down_weight, bias
    )
    output, d_first, d_first_half, g_up, g_down, g_up_bias, vecs = feed_forward(
        attended, block_input, row(out_bias), row(norm1_gain), row(norm1_bias), up_two, bias_two,
        down_two, row(down_bias), row(norm2_gain), row(norm2_bias), cotangent,
    )
    input_grad, up_sum, down_sum, late_sum, small = attention_back(
        d_first, d_first_half, x_all, segment_ids, (queries, keys, values), lse, context, qkv_two, out_two,
        g_up, g_down, g_up_bias, vecs,
    )
    ff = up_bias.shape[0]
    late_sum = late_sum.reshape(4, HEAD_DIM, -1)
    return (
        output,
        input_grad,
        jnp.swapaxes(late_sum[:3], 1, 2),
        small[6, ff : ff + 2 * HEAD_DIM].reshape(2, HEAD_DIM),
        late_sum[3],
        small[0],
        small[1],
        small[2],
        up_sum.reshape(up_weight.shape),
        small[6, :ff],
        down_sum.reshape(down_weight.shape),
        small[3],
        small[4],
        small[5],
    )


def solution(mesh):
    placed = (
        P(("dp", "tensor"), None),
        P("dp", None),
        P(None, None, "tensor"),
        P(None, "tensor"),
        P("tensor", None),
        P(),
        P(),
        P(),
        P(None, "tensor"),
        P("tensor"),
        P("tensor", None),
        P(),
        P(),
        P(),
        P(("dp", "tensor"), None),
    )
    return jax.shard_map(
        per_device,
        mesh=mesh,
        in_specs=placed,
        out_specs=(
            P(("dp", "tensor"), None),
            P(("dp", "tensor"), None),
            P(None, None, "tensor"),
            P(None, "tensor"),
            P("tensor", None),
            P(),
            P(),
            P(),
            P(None, "tensor"),
            P("tensor"),
            P("tensor", None),
            P(),
            P(),
            P(),
        ),
        check_vma=False,
    )
```

```python
import jax
import jax.numpy as jnp
from jax import lax
from jax.experimental import pallas as pl
from jax.experimental.pallas import tpu as pltpu
from jax.sharding import PartitionSpec as P

HEAD_DIM = 64
RING = 8
BLOCK = 128
HALF = 64
CHIP = 2 * BLOCK
PIECES = 8
MESH = pl.DeviceIdType.MESH
VMEM_WHOLE = pl.BlockSpec(memory_space=pltpu.VMEM)
VMEM_BYTES = 60 * 1024 * 1024
half = jnp.bfloat16
wide = jnp.float32


EPS = 1e-12
MASKED = -1e30
ROOT_HALF = 0.7071067811865476
INV_ROOT_TAU = 0.3989422804014327


def ring_place():
    t = lax.axis_index("tensor")
    dp = lax.axis_index("dp")
    base = (t // RING) * RING
    j = t % RING
    x = j // 2
    c = j % 2

    def block_of(step, other=False):
        xx = lax.rem(x + step + 4, 4)
        return xx * 2 + ((1 - c) if other else c)

    def device_of(step, other=False):
        return (dp, base + block_of(step, other))

    return block_of, device_of


def ring_order(s):
    return s + s // 2 - 2 * (s // 3)


def greet(devices):
    barrier = pltpu.get_barrier_semaphore()
    for device in devices:
        pl.semaphore_signal(barrier, inc=1, device_id=device, device_id_type=MESH)
    pl.semaphore_wait(barrier, len(devices))


def greet_ring():
    _, device_of = ring_place()
    greet((device_of(1), device_of(-1), device_of(0, True)))


def remote(src, dst, send, recv, slot, device):
    return pltpu.make_async_remote_copy(
        src_ref=src,
        dst_ref=dst,
        send_sem=send.at[slot],
        recv_sem=recv.at[slot],
        device_id=device,
        device_id_type=MESH,
    )


FIRST = pl.ds(0, HALF)
SECOND = pl.ds(HALF, HALF)


class Gather:
    slots = 13

    def __init__(self, src, out, send, recv):
        self.src, self.out, self.send, self.recv = src, out, send, recv
        self.block_of, self.device_of = ring_place()
        self.partner = self.device_of(0, True)

    def copy(self, place, slot, device):
        return remote(place, place, self.send, self.recv, slot, device)

    def start(self):
        src, at = self.src, self.out.at
        mine, right, left = self.block_of(0), self.device_of(1), self.device_of(-1)
        for part, slot, device in ((FIRST, 0, right), (SECOND, 3, left), (SECOND, 1, right), (FIRST, 2, left)):
            remote(src.at[part], at[mine, part], self.send, self.recv, slot, device).start()
        remote(src, at[mine], self.send, self.recv, 6, self.partner).start()
        self.out[pl.ds(mine, 1)] = src[...].reshape(1, *src.shape)

    def pass_on(self, slot, step, part, share_slot, device=None, device_slot=None):
        place = self.out.at[self.block_of(step), part]
        self.copy(place, slot, self.partner).wait_recv()
        if device is not None:
            self.copy(place, device_slot, device).start()
        self.copy(place, share_slot, self.partner).start()

    def shared(self, step, slots):
        for slot, part in zip(slots, (FIRST, SECOND)):
            self.copy(self.out.at[self.block_of(step, True), part], slot, self.partner).wait_recv()

    def ready(self, s):
        @pl.when(s == 0)
        def _():
            self.copy(self.out.at[self.block_of(0, True)], 6, self.partner).wait_recv()

        @pl.when(s == 1)
        def _():
            self.pass_on(0, -1, FIRST, 7, self.device_of(1), 4)
            self.pass_on(3, 1, SECOND, 10, self.device_of(-1), 5)
            self.pass_on(2, 1, FIRST, 9)
            self.pass_on(1, -1, SECOND, 8)
            self.shared(1, (9, 10))

        @pl.when(s == 2)
        def _():
            self.shared(-1, (7, 8))

        @pl.when(s == 3)
        def _():
            self.pass_on(4, 2, FIRST, 11)
            self.pass_on(5, 2, SECOND, 12)
            self.shared(2, (11, 12))

    def finish(self):
        half_place = self.out.at[0, FIRST]
        for slot in range(13):
            self.copy(self.out.at[0] if slot == 6 else half_place, slot, self.partner).wait_send()


class Scatter:
    slots = 10

    @staticmethod
    def scratch(width):
        return [
            pltpu.VMEM((RING, BLOCK, width), half),
            pltpu.VMEM((4, BLOCK, width), half),
            pltpu.VMEM((6, HALF, width), half),
            pltpu.VMEM((2, HALF, width), half),
            pltpu.VMEM((2, 2, HALF, width), half),
            pltpu.SemaphoreType.DMA((10,)),
            pltpu.SemaphoreType.DMA((10,)),
        ]

    def __init__(self, y, pair, stage, transit, final, send, recv):
        self.y, self.pair, self.stage, self.transit, self.final = y, pair, stage, transit, final
        self.send, self.recv = send, recv
        self.block_of, self.device_of = ring_place()
        self.partner = self.device_of(0, True)

    def computed(self, k):
        remote(self.y.at[self.block_of(k, True)], self.pair.at[k], self.send, self.recv, k, self.partner).start()

    def arrived(self, place, slot):
        remote(place, place, self.send, self.recv, slot, self.partner).wait_recv()

    def chip_sum(self, k, part):
        return self.y[self.block_of(k), part].astype(wide) + self.pair[k, part].astype(wide)

    def forward(self, at, value, place, slot, device):
        self.stage[at] = value.astype(half)
        remote(self.stage.at[at], place, self.send, self.recv, slot, device).start()

    def sides(self):
        self.arrived(self.pair.at[1], 1)
        self.forward(2, self.chip_sum(1, SECOND), self.final.at[0, 1], 6, self.device_of(1))
        self.arrived(self.pair.at[3], 3)
        self.forward(3, self.chip_sum(3, FIRST), self.final.at[1, 0], 7, self.device_of(-1))

    def across(self):
        self.arrived(self.pair.at[2], 2)
        self.forward(0, self.chip_sum(2, FIRST), self.transit.at[0], 4, self.device_of(1))
        self.forward(1, self.chip_sum(2, SECOND), self.transit.at[1], 5, self.device_of(-1))

    def through(self):
        self.arrived(self.transit.at[0], 4)
        value = self.chip_sum(1, FIRST) + self.transit[0].astype(wide)
        self.forward(4, value, self.final.at[0, 0], 8, self.device_of(1))
        self.arrived(self.transit.at[1], 5)
        value = self.chip_sum(3, SECOND) + self.transit[1].astype(wide)
        self.forward(5, value, self.final.at[1, 1], 9, self.device_of(-1))

    def result(self):
        self.arrived(self.pair.at[0], 0)
        for slot, place in ((6, (0, 1)), (7, (1, 0)), (8, (0, 0)), (9, (1, 1))):
            self.arrived(self.final.at[place], slot)
        final = self.final
        rows = [
            self.chip_sum(0, part) + final[0, h].astype(wide) + final[1, h].astype(wide)
            for h, part in enumerate((FIRST, SECOND))
        ]
        return jnp.concatenate(rows, axis=0)

    def finish(self):
        for slot in range(10):
            place = self.pair.at[0] if slot < 4 else self.transit.at[0]
            remote(place, place, self.send, self.recv, slot, self.partner).wait_send()


def dot_nn(left, right):
    return lax.dot_general(left, right, (((1,), (0,)), ((), ())), preferred_element_type=wide)


def dot_nt(left, right):
    return lax.dot_general(left, right, (((1,), (1,)), ((), ())), preferred_element_type=wide)


def dot_tn(left, right):
    return lax.dot_general(left, right, (((0,), (0,)), ((), ())), preferred_element_type=wide)


def layer_norm(rows, gain, shift):
    center = rows - jnp.mean(rows, axis=-1, keepdims=True)
    inverse = lax.rsqrt(jnp.mean(center * center, axis=-1, keepdims=True) + EPS)
    normed = center * inverse
    return (normed * gain + shift, normed, inverse)


def norm_back(grad, normed, inverse, gain):
    scaled = grad * gain
    return inverse * (
        scaled
        - jnp.mean(scaled, axis=-1, keepdims=True)
        - normed * jnp.mean(scaled * normed, axis=-1, keepdims=True)
    )


def gelu_parts(pre):
    cumul = 0.5 * (1.0 + lax.erf(pre * ROOT_HALF))
    return (pre * cumul, cumul + pre * jnp.exp(-0.5 * pre * pre) * INV_ROOT_TAU)


def column_sum(rows):
    return jnp.sum(rows, axis=0, keepdims=True)


def chip_rows(ref, chip):
    block = ref[pl.ds(2 * chip, 2)]
    return block.reshape(CHIP, block.shape[2])


def flat_rows(ref):
    block = ref[...]
    return block.reshape(block.shape[0] * block.shape[1], block.shape[2])


class PlaneSum:
    def __init__(self, land, full, send, recv):
        self.land, self.full, self.send, self.recv = land, full, send, recv
        t, dp = lax.axis_index("tensor"), lax.axis_index("dp")
        self.t, self.dp = t, dp

    @staticmethod
    def peer(a, r):
        t, dp = lax.axis_index("tensor"), lax.axis_index("dp")
        other = lax.rem(dp // 4 + r // 4, 2) * 4 + lax.rem(dp + r, 4)
        return other, (other, lax.rem(t + a * RING, 2 * RING))

    @staticmethod
    def peers():
        return [PlaneSum.peer(n // PIECES, n % PIECES)[1] for n in range(1, 2 * PIECES)]

    def scatter(self, grads):
        for n in range(1, 2 * PIECES):
            piece, device = self.peer(n // PIECES, n % PIECES)
            remote(grads.at[n // PIECES, piece], self.land.at[n - 1], self.send, self.recv, n - 1, device).start()

    def share(self, grads):
        total = grads[0, self.dp].astype(wide)
        for n in range(15):
            place = self.land.at[n]
            remote(place, place, self.send, self.recv, n, (self.dp, self.t)).wait_recv()
            total += self.land[n].astype(wide)
        self.full[pl.ds(self.dp, 1)] = total.astype(half).reshape(1, *total.shape)
        for r in range(1, PIECES):
            place = self.full.at[self.dp]
            remote(place, place, self.send, self.recv, 14 + r, self.peer(0, r)[1]).start()

    def result(self):
        for r in range(1, PIECES):
            piece = lax.rem(self.dp // 4 + r // 4, 2) * 4 + lax.rem(self.dp + 8 - r, 4)
            place = self.full.at[piece]
            remote(place, place, self.send, self.recv, 14 + r, (self.dp, self.t)).wait_recv()
        for n in range(22):
            place = self.land.at[0]
            remote(place, place, self.send, self.recv, n, (self.dp, self.t)).wait_send()

    @staticmethod
    def scratch(rows, width):
        return [
            pltpu.VMEM((15, rows, width), half),
            pltpu.SemaphoreType.DMA((22,)),
            pltpu.SemaphoreType.DMA((22,)),
        ]


class SmallSum:
    scratch = [
        pltpu.VMEM((8, 8, 1024), wide),
        pltpu.VMEM((2, 8, 1024), wide),
        pltpu.VMEM((15, 8, 1024), wide),
        pltpu.SemaphoreType.DMA((22,)),
        pltpu.SemaphoreType.DMA((22,)),
    ]

    def __init__(self, line, base, land, send, recv):
        self.line, self.base, self.land, self.send, self.recv = line, base, land, send, recv
        self.t, self.dp = lax.axis_index("tensor"), lax.axis_index("dp")

    @staticmethod
    def line_peer(r):
        t, dp = lax.axis_index("tensor"), lax.axis_index("dp")
        return (dp, (t // RING) * RING + lax.rem(t + r, RING))

    @staticmethod
    def peers():
        return [SmallSum.line_peer(r) for r in range(1, RING)]

    def start(self, vecs):
        for r in range(1, RING):
            remote(vecs, self.line.at[r], self.send, self.recv, 14 + r, self.line_peer(r)).start()

    def plane(self, vecs, shard_rows):
        total = vecs[...]
        for r in range(1, RING):
            place = self.line.at[r]
            remote(place, place, self.send, self.recv, 14 + r, (self.dp, self.t)).wait_recv()
            total += self.line[r]
        row = lax.broadcasted_iota(jnp.int32, total.shape, 0)
        for a in range(2):
            self.base[a] = jnp.where(row == 6, jnp.broadcast_to(shard_rows[a], total.shape), total)
        for n in range(1, 2 * PIECES):
            _, device = PlaneSum.peer(n // PIECES, n % PIECES)
            remote(self.base.at[n // PIECES], self.land.at[n - 1], self.send, self.recv, n - 1, device).start()

    def result(self):
        total = self.base[0]
        for n in range(15):
            place = self.land.at[n]
            remote(place, place, self.send, self.recv, n, (self.dp, self.t)).wait_recv()
            total += self.land[n]
        for n in range(22):
            place = self.land.at[0]
            remote(place, place, self.send, self.recv, n, (self.dp, self.t)).wait_send()
        return total


def segment_column(ids, column):
    upper = lax.axis_index("tensor") // RING
    numbers = jnp.where(upper == 0, ids[pl.ds(0, 1)], ids[pl.ds(1, 1)])
    column[...] = jnp.transpose(jnp.broadcast_to(numbers, (128, numbers.shape[1])))
    return numbers


def put_term(scatter, chip, term):
    scatter.y[pl.ds(2 * chip, 2)] = term.astype(half).reshape(2, BLOCK, term.shape[1])


def layer_kernel(
    x, ids, qkv, qv_bias, out_weight, out_bias, gain1, bias1, up, up_bias, down, down_bias, gain2, bias2, cot,
    out, input_grad, up_full, down_full, late_full, small_out,
    x_all, hidden_all, d_second_all, d_first_all, own_rows, hidden, normed_one, d_second,
    queries, keys, values, lse, context, column,
    qkv_two, qv_bias_two, out_two, up_two, up_bias_two, down_two,
    act, slope, d_pre, g_up, g_down, g_up_bias, vecs,
    d_keys, d_values, d_qkv, query_sum, late,
    gather_sems, trade_sems, *scratch,
):
    block_of, device_of = ring_place()
    shard = up.shape[1]
    group = 3 * HEAD_DIM
    scatters = [Scatter(*scratch[7 * i : 7 * i + 7]) for i in range(4)]
    scratch = scratch[28:]
    small, scratch = SmallSum(*scratch[:5]), scratch[5:]
    up_plane, down_plane, late_plane = (
        PlaneSum(scratch[3 * i], full, scratch[3 * i + 1], scratch[3 * i + 2])
        for i, full in enumerate((up_full, down_full, late_full))
    )

    def gather_of(i, src, dst):
        return Gather(src, dst, gather_sems.at[2 * i], gather_sems.at[2 * i + 1])

    greet(PlaneSum.peers() + SmallSum.peers())

    gather = gather_of(0, x, x_all)
    gather.start()
    across_z = PlaneSum.peer(1, 0)[1]
    pairs = (
        (qv_bias, qv_bias_two), (qkv, qkv_two), (out_weight, out_two),
        (up_bias, up_bias_two), (up, up_two), (down, down_two),
    )
    trades = [
        remote(mine, two.at[1], trade_sems.at[0], trade_sems.at[1], slot, across_z)
        for slot, (mine, two) in enumerate(pairs)
    ]
    for trade in trades:
        trade.start()
    for mine, two in pairs:
        two[0] = mine[...]
    numbers = segment_column(ids, column)

    def project(a, chip):
        rows = pl.ds(chip * CHIP, CHIP)
        product = dot_nt(chip_rows(x_all, chip), qkv_two[a].reshape(group, x.shape[1]))
        parts = [product[:, i * HEAD_DIM : (i + 1) * HEAD_DIM] for i in range(3)]
        queries[a, rows] = (parts[0] + qv_bias_two[a, 0:1]).astype(half)
        keys[a, rows] = parts[1].astype(half)
        values[a, rows] = (parts[2] + qv_bias_two[a, 1:2]).astype(half)

    @pl.loop(0, 4)
    def _(s):
        gather.ready(s)
        project(0, block_of(ring_order(s)) // 2)

    trades[0].wait_recv()
    trades[1].wait_recv()

    @pl.loop(0, 4)
    def _(chip):
        project(1, chip)

    trades[2].wait_recv()
    scatter = scatters[0]

    @pl.loop(0, 4)
    def _(i):
        k = ring_order(3 - i)
        chip = block_of(k) // 2
        rows = pl.ds(chip * CHIP, CHIP)
        allowed = column[rows, 0:1] == numbers
        for a in range(2):
            scores = dot_nt(queries[a, rows] * HEAD_DIM ** (-0.5), keys[a])
            masked = jnp.where(allowed, scores, MASKED)
            top = jnp.max(masked, axis=-1, keepdims=True)
            weights = jnp.exp(masked - top)
            mass = jnp.sum(weights, axis=-1, keepdims=True)
            lse[a, rows] = top + jnp.log(mass)
            probs = (weights * (1.0 / mass)).astype(half)
            context[rows, a * HEAD_DIM : (a + 1) * HEAD_DIM] = dot_nn(probs, values[a]).astype(half)
        put_term(scatter, chip, dot_nn(context[rows], flat_rows(out_two)))
        scatter.computed(k)

        @pl.when(i == 1)
        def _():
            scatter.across()

    scatter.sides()
    scatter.through()
    first = x[...].astype(wide) + scatter.result() + out_bias[...]
    normal, normed, inverse_one = layer_norm(first, gain1[...], bias1[...])
    own_rows[0] = normal.astype(half)

    gather = gather_of(1, own_rows.at[0], hidden_all)
    gather.start()
    hidden[...] = normal
    normed_one[...] = normed
    scatter = scatters[1]
    for trade in trades[3:]:
        trade.wait_recv()

    @pl.loop(0, 4)
    def _(s):
        @pl.when(s == 3)
        def _():
            scatter.sides()

        gather.ready(s)
        k = ring_order(s)
        chip = block_of(k) // 2
        rows = pl.ds(chip * CHIP, CHIP)
        for a in range(2):
            pre = dot_nn(chip_rows(hidden_all, chip), up_two[a]) + up_bias_two[a]
            value, gelu_slope = gelu_parts(pre)
            act[rows, a * shard : (a + 1) * shard] = value.astype(half)
            slope[rows, a * shard : (a + 1) * shard] = gelu_slope
        put_term(scatter, chip, dot_nn(act[rows], flat_rows(down_two)))
        scatter.computed(k)

    scatter.across()
    scatter.through()
    second = hidden[...] + scatter.result() + down_bias[...]
    output, normed_two, inverse_two = layer_norm(second, gain2[...], bias2[...])
    grad = cot[...].astype(wide)
    grad_second = norm_back(grad, normed_two, inverse_two, gain2[...])
    own_rows[1] = grad_second.astype(half)

    gather = gather_of(2, own_rows.at[1], d_second_all)
    gather.start()
    d_second[...] = grad_second
    out[...] = output.astype(half)
    vecs[pl.ds(3, 1)] = column_sum(grad_second)
    vecs[pl.ds(4, 1)] = column_sum(grad * normed_two)
    vecs[pl.ds(5, 1)] = column_sum(grad)
    vecs[pl.ds(6, 2)] = jnp.zeros((2, grad.shape[1]), wide)
    g_up_bias[...] = jnp.zeros_like(g_up_bias)
    scatter = scatters[2]

    @pl.loop(0, 4)
    def _(s):
        @pl.when(s == 3)
        def _():
            scatter.sides()

        gather.ready(s)
        k = ring_order(s)
        chip = block_of(k) // 2
        rows = pl.ds(chip * CHIP, CHIP)
        grad_pre = dot_nt(chip_rows(d_second_all, chip), flat_rows(down_two)) * slope[rows]
        g_up_bias[...] += column_sum(grad_pre)
        grad_pre = grad_pre.astype(half)
        d_pre[rows] = grad_pre
        put_term(scatter, chip, dot_nt(grad_pre[:, :shard], up_two[0]) + dot_nt(grad_pre[:, shard:], up_two[1]))
        scatter.computed(k)

    scatter.across()
    for a in range(2):
        part = dot_tn(act[:, a * shard : (a + 1) * shard], flat_rows(d_second_all)).astype(half)
        g_down[a] = part.reshape(PIECES, shard // PIECES, part.shape[1])
    down_plane.scatter(g_down)
    scatter.through()

    @pl.loop(0, 4)
    def _(i):
        columns = pl.ds(pl.multiple_of(i * 256, 256), 256)
        left = hidden_all[:, :, columns].reshape(RING * BLOCK, 256)
        part = dot_tn(left, d_pre[...]).astype(half)
        for a in range(2):
            g_up[a, pl.ds(2 * i, 2)] = part[:, a * shard : (a + 1) * shard].reshape(2, BLOCK, shard)

    d_hidden = d_second[...] + scatter.result()
    grad_first = norm_back(d_hidden, normed_one[...], inverse_one, gain1[...])
    own_rows[2] = grad_first.astype(half)

    gather = gather_of(3, own_rows.at[2], d_first_all)
    gather.start()
    up_plane.scatter(g_up)
    vecs[pl.ds(0, 1)] = column_sum(grad_first)
    vecs[pl.ds(1, 1)] = column_sum(d_hidden * normed_one[...])
    vecs[pl.ds(2, 1)] = column_sum(d_hidden)
    hidden[...] = grad_first
    small.start(vecs)
    d_keys[...] = jnp.zeros_like(d_keys)
    d_values[...] = jnp.zeros_like(d_values)
    query_sum[...] = jnp.zeros_like(query_sum)

    @pl.loop(0, 4)
    def _(s):
        gather.ready(s)
        chip = block_of(ring_order(s)) // 2
        rows = pl.ds(chip * CHIP, CHIP)
        d_context = dot_nt(chip_rows(d_first_all, chip), flat_rows(out_two)).astype(half)
        allowed = column[rows, 0:1] == numbers
        for a in range(2):
            d_head = d_context[:, a * HEAD_DIM : (a + 1) * HEAD_DIM]
            query = queries[a, rows]
            scores = dot_nt(query * HEAD_DIM ** (-0.5), keys[a])
            probs = jnp.exp(jnp.where(allowed, scores, MASKED) - lse[a, rows])
            d_values[a] += dot_tn(d_head, probs.astype(half))
            d_probs = dot_nt(d_head * HEAD_DIM ** (-0.5), values[a])
            mean = jnp.sum(probs * d_probs, axis=-1, keepdims=True)
            d_scores = (probs * (d_probs - mean)).astype(half)
            d_query = dot_nn(d_scores, keys[a])
            query_sum[a] += column_sum(d_query)
            d_qkv[rows, a * group : a * group + HEAD_DIM] = d_query.astype(half)
            d_keys[a] += dot_tn(query, d_scores)

    shard_rows = []
    for a in range(2):
        at = a * group + HEAD_DIM
        d_qkv[:, at : at + HEAD_DIM] = jnp.transpose(d_keys[a].astype(half))
        d_qkv[:, at + HEAD_DIM : at + 2 * HEAD_DIM] = jnp.transpose(d_values[a].astype(half))
        value_sum = jnp.sum(d_values[a], axis=1, keepdims=True)
        value_sum = jnp.transpose(jnp.broadcast_to(value_sum, (HEAD_DIM, 128)))[0:1]
        shard_rows.append(
            jnp.concatenate(
                [
                    g_up_bias[:, a * shard : (a + 1) * shard],
                    query_sum[a],
                    value_sum,
                    jnp.zeros((1, vecs.shape[1] - shard - 2 * HEAD_DIM), wide),
                ],
                axis=1,
            )
        )
    grad_out = dot_tn(context[...], flat_rows(d_first_all)).astype(half)
    piece = late.shape[2]
    for a in range(2):
        part = dot_tn(d_qkv[:, a * group : (a + 1) * group], flat_rows(x_all)).astype(half)
        late[a, pl.ds(0, 6)] = part.reshape(6, piece, part.shape[1])
        part = grad_out[a * HEAD_DIM : (a + 1) * HEAD_DIM]
        late[a, pl.ds(6, 2)] = part.reshape(2, piece, part.shape[1])
    late_plane.scatter(late)
    small.plane(vecs, shard_rows)
    scatter = scatters[3]

    @pl.loop(0, 4)
    def _(i):
        k = ring_order(3 - i)
        chip = block_of(k) // 2
        weight = qkv_two[...].reshape(2 * group, x.shape[1])
        put_term(scatter, chip, dot_nn(d_qkv[pl.ds(chip * CHIP, CHIP)], weight))
        scatter.computed(k)

        @pl.when(i == 1)
        def _():
            scatter.across()

    scatter.sides()
    down_plane.share(g_down)
    scatter.through()
    up_plane.share(g_up)
    input_grad[...] = (hidden[...] + scatter.result()).astype(half)
    late_plane.share(late)
    for plane in (down_plane, up_plane, late_plane):
        plane.result()
    small_out[...] = small.result()
    for i, (src, dst) in enumerate(((x, x_all), (x, hidden_all), (x, d_second_all), (x, d_first_all))):
        gather_of(i, src, dst).finish()
    for scatter in scatters:
        scatter.finish()
    for trade in trades:
        trade.wait_send()


def layer(x, ids, qkv, qv_bias, out_weight, out_bias, gain1, bias1, up, up_bias, down, down_bias, gain2, bias2, cot):
    rows, width = x.shape
    tokens = RING * rows
    shard = up.shape[1]
    late = (PIECES, 4 * HEAD_DIM // PIECES, width)
    up_pieces = (PIECES, width // PIECES, shard)
    down_pieces = (PIECES, shard // PIECES, width)
    gathered = pltpu.VMEM((RING, rows, width), half)
    full_rows = pltpu.VMEM((rows, width), wide)
    head = pltpu.VMEM((2, tokens, HEAD_DIM), half)
    ff = pltpu.VMEM((tokens, 2 * shard), half)
    turned = pltpu.VMEM((2, HEAD_DIM, tokens), wide)
    scratch = [gathered] * 4 + [pltpu.VMEM((3, rows, width), half)] + [full_rows] * 3
    scratch += [head] * 3
    scratch += [
        pltpu.VMEM((2, tokens, 1), wide),
        pltpu.VMEM((tokens, 2 * HEAD_DIM), half),
        pltpu.VMEM((tokens, 128), jnp.int32),
    ]
    scratch += [pltpu.VMEM((2, *arr.shape), arr.dtype) for arr in (qkv, qv_bias, out_weight, up, up_bias, down)]
    scratch += [ff, pltpu.VMEM((tokens, 2 * shard), wide), ff]
    scratch += [pltpu.VMEM((2, *up_pieces), half), pltpu.VMEM((2, *down_pieces), half)]
    scratch += [pltpu.VMEM((1, 2 * shard), wide), pltpu.VMEM((8, width), wide)]
    scratch += [turned, turned, pltpu.VMEM((tokens, 6 * HEAD_DIM), half), pltpu.VMEM((2, 1, HEAD_DIM), wide)]
    scratch += [pltpu.VMEM((2, *late), half)]
    scratch += [pltpu.SemaphoreType.DMA((8, Gather.slots)), pltpu.SemaphoreType.DMA((2, 6))]
    scratch += Scatter.scratch(width) * 4 + SmallSum.scratch
    for pieces in (up_pieces, down_pieces, late):
        scratch += PlaneSum.scratch(*pieces[1:])
    return pl.pallas_call(
        layer_kernel,
        out_shape=(
            jax.ShapeDtypeStruct((rows, width), half),
            jax.ShapeDtypeStruct((rows, width), half),
            jax.ShapeDtypeStruct(up_pieces, half),
            jax.ShapeDtypeStruct(down_pieces, half),
            jax.ShapeDtypeStruct(late, half),
            jax.ShapeDtypeStruct((8, width), wide),
        ),
        in_specs=[VMEM_WHOLE] * 15,
        out_specs=(VMEM_WHOLE,) * 6,
        scratch_shapes=scratch,
        compiler_params=pltpu.CompilerParams(
            collective_id=0, has_side_effects=True, vmem_limit_bytes=VMEM_BYTES
        ),
    )(x, ids, qkv, qv_bias, out_weight, out_bias, gain1, bias1, up, up_bias, down, down_bias, gain2, bias2, cot)


def outputs_kernel(
    out_in, grad_in, up_full, down_full, late_full, small,
    out, input_grad, g_qkv, g_qv_bias, g_out, g_out_bias, g_gain1, g_bias1, g_up, g_up_bias, g_down, g_down_bias,
    g_gain2, g_bias2,
):
    out[...] = out_in[...]
    input_grad[...] = grad_in[...]
    g_up[...] = flat_rows(up_full).astype(wide)
    g_down[...] = flat_rows(down_full).astype(wide)
    late = flat_rows(late_full).astype(wide).reshape(4, HEAD_DIM, out.shape[1])
    g_qkv[...] = late[:3]
    g_out[...] = late[3]
    for i, ref in enumerate((g_out_bias, g_gain1, g_bias1, g_down_bias, g_gain2, g_bias2)):
        ref[...] = small[pl.ds(i, 1)]
    ff = g_up_bias.shape[1]
    g_up_bias[...] = small[pl.ds(6, 1), 0:ff]
    for i in range(2):
        g_qv_bias[pl.ds(i, 1)] = small[pl.ds(6, 1), ff + i * HEAD_DIM : ff + (i + 1) * HEAD_DIM]


def write_outputs(results):
    rows, width = results[0].shape
    ff = results[2].shape[2]
    vector = jax.ShapeDtypeStruct((1, width), wide)
    block = jax.ShapeDtypeStruct((rows, width), half)
    return pl.pallas_call(
        outputs_kernel,
        out_shape=(
            block,
            block,
            jax.ShapeDtypeStruct((3, HEAD_DIM, width), wide),
            jax.ShapeDtypeStruct((2, HEAD_DIM), wide),
            jax.ShapeDtypeStruct((HEAD_DIM, width), wide),
            vector,
            vector,
            vector,
            jax.ShapeDtypeStruct((width, ff), wide),
            jax.ShapeDtypeStruct((1, ff), wide),
            jax.ShapeDtypeStruct((ff, width), wide),
            vector,
            vector,
            vector,
        ),
        in_specs=[VMEM_WHOLE] * 6,
        out_specs=(VMEM_WHOLE,) * 14,
    )(*results)


def row(vector):
    return vector.reshape(1, vector.shape[0])


def per_device(
    block_input,
    segment_ids,
    qkv_weight,
    qv_bias,
    out_weight,
    out_bias,
    norm1_gain,
    norm1_bias,
    up_weight,
    up_bias,
    down_weight,
    down_bias,
    norm2_gain,
    norm2_bias,
    cotangent,
):
    results = layer(
        block_input, segment_ids, jnp.swapaxes(qkv_weight, 1, 2), qv_bias, out_weight, row(out_bias),
        row(norm1_gain), row(norm1_bias), up_weight, row(up_bias), down_weight, row(down_bias),
        row(norm2_gain), row(norm2_bias), cotangent,
    )
    out, input_grad, g_qkv, g_qv_bias, g_out, *vectors = write_outputs(results)
    g_out_bias, g_gain1, g_bias1, g_up, g_up_bias, g_down, g_down_bias, g_gain2, g_bias2 = (
        arr.reshape(-1) if arr.shape[0] == 1 else arr for arr in vectors
    )
    return (
        out, input_grad, jnp.swapaxes(g_qkv, 1, 2), g_qv_bias, g_out, g_out_bias, g_gain1, g_bias1,
        g_up, g_up_bias, g_down, g_down_bias, g_gain2, g_bias2,
    )


def solution(mesh):
    placed = (
        P(("dp", "tensor"), None),
        P("dp", None),
        P(None, None, "tensor"),
        P(None, "tensor"),
        P("tensor", None),
        P(),
        P(),
        P(),
        P(None, "tensor"),
        P("tensor"),
        P("tensor", None),
        P(),
        P(),
        P(),
        P(("dp", "tensor"), None),
    )
    return jax.shard_map(
        per_device,
        mesh=mesh,
        in_specs=placed,
        out_specs=(
            P(("dp", "tensor"), None),
            P(("dp", "tensor"), None),
            P(None, None, "tensor"),
            P(None, "tensor"),
            P("tensor", None),
            P(),
            P(),
            P(),
            P(None, "tensor"),
            P("tensor"),
            P("tensor", None),
            P(),
            P(),
            P(),
        ),
        check_vma=False,
    )
```

```python
import jax
import jax.numpy as jnp
from jax import lax
from jax.experimental import pallas as pl
from jax.experimental.pallas import tpu as pltpu
from jax.sharding import PartitionSpec as P

HEAD_DIM = 64
RING = 8
BLOCK = 128
HALF = 64
CHIP = 2 * BLOCK
PIECES = 8
MESH = pl.DeviceIdType.MESH
VMEM_WHOLE = pl.BlockSpec(memory_space=pltpu.VMEM)
VMEM_BYTES = 60 * 1024 * 1024
half = jnp.bfloat16
wide = jnp.float32


EPS = 1e-12
MASKED = -1e30
ROOT_HALF = 0.7071067811865476
INV_ROOT_TAU = 0.3989422804014327


def ring_place():
    t = lax.axis_index("tensor")
    dp = lax.axis_index("dp")
    base = (t // RING) * RING
    j = t % RING
    x = j // 2
    c = j % 2

    def block_of(step, other=False):
        xx = lax.rem(x + step + 4, 4)
        return xx * 2 + ((1 - c) if other else c)

    def device_of(step, other=False):
        return (dp, base + block_of(step, other))

    return block_of, device_of


def ring_order(s):
    return s + s // 2 - 2 * (s // 3)


def greet(devices):
    barrier = pltpu.get_barrier_semaphore()
    for device in devices:
        pl.semaphore_signal(barrier, inc=1, device_id=device, device_id_type=MESH)
    pl.semaphore_wait(barrier, len(devices))


def greet_ring():
    _, device_of = ring_place()
    greet((device_of(1), device_of(-1), device_of(0, True)))


def remote(src, dst, send, recv, slot, device):
    return pltpu.make_async_remote_copy(
        src_ref=src,
        dst_ref=dst,
        send_sem=send.at[slot],
        recv_sem=recv.at[slot],
        device_id=device,
        device_id_type=MESH,
    )


FIRST = pl.ds(0, HALF)
SECOND = pl.ds(HALF, HALF)


class Gather:
    slots = 13

    def __init__(self, src, out, send, recv):
        self.src, self.out, self.send, self.recv = src, out, send, recv
        self.block_of, self.device_of = ring_place()
        self.partner = self.device_of(0, True)

    def copy(self, place, slot, device):
        return remote(place, place, self.send, self.recv, slot, device)

    def start(self):
        src, at = self.src, self.out.at
        mine, right, left = self.block_of(0), self.device_of(1), self.device_of(-1)
        for part, slot, device in ((FIRST, 0, right), (SECOND, 3, left), (SECOND, 1, right), (FIRST, 2, left)):
            remote(src.at[part], at[mine, part], self.send, self.recv, slot, device).start()
        remote(src, at[mine], self.send, self.recv, 6, self.partner).start()
        self.out[pl.ds(mine, 1)] = src[...].reshape(1, *src.shape)

    def pass_on(self, slot, step, part, share_slot, device=None, device_slot=None):
        place = self.out.at[self.block_of(step), part]
        self.copy(place, slot, self.partner).wait_recv()
        if device is not None:
            self.copy(place, device_slot, device).start()
        self.copy(place, share_slot, self.partner).start()

    def shared(self, step, slots):
        for slot, part in zip(slots, (FIRST, SECOND)):
            self.copy(self.out.at[self.block_of(step, True), part], slot, self.partner).wait_recv()

    def ready(self, s):
        @pl.when(s == 0)
        def _():
            self.copy(self.out.at[self.block_of(0, True)], 6, self.partner).wait_recv()

        @pl.when(s == 1)
        def _():
            self.pass_on(0, -1, FIRST, 7, self.device_of(1), 4)
            self.pass_on(3, 1, SECOND, 10, self.device_of(-1), 5)
            self.pass_on(2, 1, FIRST, 9)
            self.pass_on(1, -1, SECOND, 8)
            self.shared(1, (9, 10))

        @pl.when(s == 2)
        def _():
            self.shared(-1, (7, 8))

        @pl.when(s == 3)
        def _():
            self.pass_on(4, 2, FIRST, 11)
            self.pass_on(5, 2, SECOND, 12)
            self.shared(2, (11, 12))

    def finish(self):
        half_place = self.out.at[0, FIRST]
        for slot in range(13):
            self.copy(self.out.at[0] if slot == 6 else half_place, slot, self.partner).wait_send()


class Scatter:
    slots = 10

    @staticmethod
    def scratch(width):
        return [
            pltpu.VMEM((RING, BLOCK, width), half),
            pltpu.VMEM((4, BLOCK, width), half),
            pltpu.VMEM((6, HALF, width), half),
            pltpu.VMEM((2, HALF, width), half),
            pltpu.VMEM((2, 2, HALF, width), half),
            pltpu.SemaphoreType.DMA((10,)),
            pltpu.SemaphoreType.DMA((10,)),
        ]

    def __init__(self, y, pair, stage, transit, final, send, recv):
        self.y, self.pair, self.stage, self.transit, self.final = y, pair, stage, transit, final
        self.send, self.recv = send, recv
        self.block_of, self.device_of = ring_place()
        self.partner = self.device_of(0, True)

    def computed(self, k):
        remote(self.y.at[self.block_of(k, True)], self.pair.at[k], self.send, self.recv, k, self.partner).start()

    def arrived(self, place, slot):
        remote(place, place, self.send, self.recv, slot, self.partner).wait_recv()

    def chip_sum(self, k, part):
        return self.y[self.block_of(k), part].astype(wide) + self.pair[k, part].astype(wide)

    def forward(self, at, value, place, slot, device):
        self.stage[at] = value.astype(half)
        remote(self.stage.at[at], place, self.send, self.recv, slot, device).start()

    def sides(self):
        self.arrived(self.pair.at[1], 1)
        self.forward(2, self.chip_sum(1, SECOND), self.final.at[0, 1], 6, self.device_of(1))
        self.arrived(self.pair.at[3], 3)
        self.forward(3, self.chip_sum(3, FIRST), self.final.at[1, 0], 7, self.device_of(-1))

    def across(self):
        self.arrived(self.pair.at[2], 2)
        self.forward(0, self.chip_sum(2, FIRST), self.transit.at[0], 4, self.device_of(1))
        self.forward(1, self.chip_sum(2, SECOND), self.transit.at[1], 5, self.device_of(-1))

    def through(self):
        self.arrived(self.transit.at[0], 4)
        value = self.chip_sum(1, FIRST) + self.transit[0].astype(wide)
        self.forward(4, value, self.final.at[0, 0], 8, self.device_of(1))
        self.arrived(self.transit.at[1], 5)
        value = self.chip_sum(3, SECOND) + self.transit[1].astype(wide)
        self.forward(5, value, self.final.at[1, 1], 9, self.device_of(-1))

    def result(self):
        self.arrived(self.pair.at[0], 0)
        for slot, place in ((6, (0, 1)), (7, (1, 0)), (8, (0, 0)), (9, (1, 1))):
            self.arrived(self.final.at[place], slot)
        final = self.final
        rows = [
            self.chip_sum(0, part) + final[0, h].astype(wide) + final[1, h].astype(wide)
            for h, part in enumerate((FIRST, SECOND))
        ]
        return jnp.concatenate(rows, axis=0)

    def finish(self):
        for slot in range(10):
            place = self.pair.at[0] if slot < 4 else self.transit.at[0]
            remote(place, place, self.send, self.recv, slot, self.partner).wait_send()


def dot_nn(left, right):
    return lax.dot_general(left, right, (((1,), (0,)), ((), ())), preferred_element_type=wide)


def dot_nt(left, right):
    return lax.dot_general(left, right, (((1,), (1,)), ((), ())), preferred_element_type=wide)


def dot_tn(left, right):
    return lax.dot_general(left, right, (((0,), (0,)), ((), ())), preferred_element_type=wide)


def layer_norm(rows, gain, shift):
    center = rows - jnp.mean(rows, axis=-1, keepdims=True)
    inverse = lax.rsqrt(jnp.mean(center * center, axis=-1, keepdims=True) + EPS)
    normed = center * inverse
    return (normed * gain + shift, normed, inverse)


def norm_back(grad, normed, inverse, gain):
    scaled = grad * gain
    return inverse * (
        scaled
        - jnp.mean(scaled, axis=-1, keepdims=True)
        - normed * jnp.mean(scaled * normed, axis=-1, keepdims=True)
    )


def gelu_parts(pre):
    cumul = 0.5 * (1.0 + lax.erf(pre * ROOT_HALF))
    return (pre * cumul, cumul + pre * jnp.exp(-0.5 * pre * pre) * INV_ROOT_TAU)


def column_sum(rows):
    return jnp.sum(rows, axis=0, keepdims=True)


def chip_rows(ref, chip):
    block = ref[pl.ds(2 * chip, 2)]
    return block.reshape(CHIP, block.shape[2])


def flat_rows(ref):
    block = ref[...]
    return block.reshape(block.shape[0] * block.shape[1], block.shape[2])


class PlaneSum:
    def __init__(self, land, full, send, recv):
        self.land, self.full, self.send, self.recv = land, full, send, recv
        t, dp = lax.axis_index("tensor"), lax.axis_index("dp")
        self.t, self.dp = t, dp

    @staticmethod
    def peer(a, r):
        t, dp = lax.axis_index("tensor"), lax.axis_index("dp")
        other = lax.rem(dp // 4 + r // 4, 2) * 4 + lax.rem(dp + r, 4)
        return other, (other, lax.rem(t + a * RING, 2 * RING))

    @staticmethod
    def peers():
        return [PlaneSum.peer(n // PIECES, n % PIECES)[1] for n in range(1, 2 * PIECES)]

    def hand_out(self, total):
        self.full[pl.ds(self.dp, 1)] = total.astype(half).reshape(1, *total.shape)
        for r in range(1, PIECES):
            place = self.full.at[self.dp]
            remote(place, place, self.send, self.recv, 14 + r, self.peer(0, r)[1]).start()

    def result(self):
        for r in range(1, PIECES):
            piece = lax.rem(self.dp // 4 + r // 4, 2) * 4 + lax.rem(self.dp + 8 - r, 4)
            place = self.full.at[piece]
            remote(place, place, self.send, self.recv, 14 + r, (self.dp, self.t)).wait_recv()
        self.sent()


class TwoLevelSum(PlaneSum):
    def __init__(self, z_first, near, mid, far, full, send, recv):
        super().__init__(far, full, send, recv)
        self.z_first, self.near, self.mid = z_first, near, mid

    @staticmethod
    def peer_z(n):
        dp, t = lax.axis_index("dp"), lax.axis_index("tensor")
        z_lo = lax.rem(dp // 4 + n % 2, 2)
        return z_lo, (z_lo * 4 + lax.rem(dp, 4), lax.rem(t + (n // 2) * RING, 2 * RING))

    @staticmethod
    def peer_y(r):
        dp, t = lax.axis_index("dp"), lax.axis_index("tensor")
        y = lax.rem(dp + r, 4)
        return y, ((dp // 4) * 4 + y, t)

    def here(self):
        return (self.dp, self.t)

    def scatter(self, grads):
        for n in range(1, 4):
            if self.z_first:
                z_lo, device = self.peer_z(n)
                remote(grads.at[n // 2, pl.ds(4 * z_lo, 4)], self.near.at[n - 1], self.send, self.recv, n - 1, device).start()
            else:
                y, device = self.peer_y(n)
                for m in range(4):
                    source = grads.at[m // 2, 4 * (m % 2) + y]
                    remote(source, self.near.at[n - 1, m], self.send, self.recv, 4 * (n - 1) + m, device).start()

    def turn(self, grads):
        count = 3 if self.z_first else 12
        for slot in range(count):
            place = self.near.at[slot] if self.z_first else self.near.at[slot // 4, slot % 4]
            remote(place, place, self.send, self.recv, slot, self.here()).wait_recv()
        y, z_lo = lax.rem(self.dp, 4), self.dp // 4
        for m in range(4):
            mine = grads[0, 4 * z_lo + m] if self.z_first else grads[m // 2, 4 * (m % 2) + y]
            total = mine.astype(wide)
            for n in range(3):
                total += self.near[n, m].astype(wide)
            self.mid[m] = total.astype(half)
        for n in range(1, 4):
            if self.z_first:
                at, device = self.peer_y(n)
            else:
                z_lo_there, device = self.peer_z(n)
                at = 2 * (n // 2) + z_lo_there
            remote(self.mid.at[at], self.land.at[n - 1], self.send, self.recv, 11 + n, device).start()

    def share(self):
        at = lax.rem(self.dp, 4) if self.z_first else self.dp // 4
        total = self.mid[at].astype(wide)
        for n in range(3):
            place = self.land.at[n]
            remote(place, place, self.send, self.recv, 12 + n, self.here()).wait_recv()
            total += self.land[n].astype(wide)
        self.hand_out(total)

    def sent(self):
        for slot in range(3 if self.z_first else 12):
            place = self.near.at[0] if self.z_first else self.near.at[0, 0]
            remote(place, place, self.send, self.recv, slot, self.here()).wait_send()
        for slot in range(12, 22):
            place = self.land.at[0]
            remote(place, place, self.send, self.recv, slot, self.here()).wait_send()

    @staticmethod
    def scratch(rows, width):
        return [
            pltpu.VMEM((3, 4, rows, width), half),
            pltpu.VMEM((4, rows, width), half),
            pltpu.VMEM((3, rows, width), half),
            pltpu.SemaphoreType.DMA((22,)),
            pltpu.SemaphoreType.DMA((22,)),
        ]


class SmallSum:
    scratch = [
        pltpu.VMEM((RING, 8, 128), wide),
        pltpu.VMEM((2, 16, 128), wide),
        pltpu.VMEM((15, 16, 128), wide),
        pltpu.SemaphoreType.DMA((29,)),
        pltpu.SemaphoreType.DMA((29,)),
    ]

    def __init__(self, line, base, land, send, recv):
        self.line, self.base, self.land, self.send, self.recv = line, base, land, send, recv
        self.t, self.dp = lax.axis_index("tensor"), lax.axis_index("dp")

    @staticmethod
    def line_peer(r):
        t, dp = lax.axis_index("tensor"), lax.axis_index("dp")
        return (dp, (t // RING) * RING + lax.rem(t + r, RING))

    @staticmethod
    def peers():
        return [SmallSum.line_peer(r) for r in range(1, RING)]

    def slab(self, ref, r):
        return ref.at[:, pl.ds(pl.multiple_of(lax.rem(self.t + r, RING) * 128, 128), 128)]

    def arrived(self, place, slot):
        remote(place, place, self.send, self.recv, slot, (self.dp, self.t)).wait_recv()

    def start(self, vecs):
        for r in range(1, RING):
            remote(self.slab(vecs, r), self.line.at[r], self.send, self.recv, 14 + r, self.line_peer(r)).start()

    def plane(self, vecs, shards):
        total = self.slab(vecs, 0)[...]
        for r in range(1, RING):
            self.arrived(self.line.at[r], 14 + r)
            total += self.line[r]
        for a in range(2):
            self.base[a, 0:8] = total
            self.base[a, 8:16] = shards[a]
        for n in range(1, 2 * PIECES):
            _, device = PlaneSum.peer(n // PIECES, n % PIECES)
            remote(self.base.at[n // PIECES], self.land.at[n - 1], self.send, self.recv, n - 1, device).start()

    def share(self, sums, shard_sums):
        total = self.base[0]
        for n in range(15):
            self.arrived(self.land.at[n], n)
            total += self.land[n]
        mine = self.slab(sums, 0)
        mine[...] = total[0:8]
        shard_sums[...] = total[8:16]
        for r in range(1, RING):
            remote(mine, mine, self.send, self.recv, 21 + r, self.line_peer(r)).start()

    def finish(self, sums):
        for r in range(1, RING):
            self.arrived(self.slab(sums, RING - r), 21 + r)
        for slot in range(29):
            place = self.land.at[0] if slot < 15 else self.line.at[0]
            remote(place, place, self.send, self.recv, slot, (self.dp, self.t)).wait_send()


def segment_column(ids, column):
    upper = lax.axis_index("tensor") // RING
    numbers = jnp.where(upper == 0, ids[pl.ds(0, 1)], ids[pl.ds(1, 1)])
    column[...] = jnp.transpose(jnp.broadcast_to(numbers, (128, numbers.shape[1])))
    return numbers


def put_term(scatter, chip, term):
    scatter.y[pl.ds(2 * chip, 2)] = term.astype(half).reshape(2, BLOCK, term.shape[1])


def layer_kernel(
    x, ids, qkv, qv_bias, out_weight, out_bias, gain1, bias1, up, up_bias, down, down_bias, gain2, bias2, cot,
    out, input_grad, up_full, down_full, query_full, pair_full, out_full, sums, shard_sums,
    x_all, hidden_all, d_second_all, d_first_all, own_rows, hidden, normed_one, d_second,
    queries, keys, values, lse, context, column,
    qkv_two, qv_bias_two, out_two, up_two, up_bias_two, down_two,
    act, slope, d_pre, g_up, g_down, g_up_bias, vecs,
    d_keys, d_values, d_qkv, query_sum, g_query, g_pair, g_out,
    gather_sems, trade_sems, *scratch,
):
    block_of, device_of = ring_place()
    shard = up.shape[1]
    group = 3 * HEAD_DIM
    scatters = [Scatter(*scratch[7 * i : 7 * i + 7]) for i in range(4)]
    scratch = scratch[28:]
    small, scratch = SmallSum(*scratch[:5]), scratch[5:]
    up_plane = TwoLevelSum(False, *scratch[0:3], up_full, *scratch[3:5])
    down_plane = TwoLevelSum(True, *scratch[5:8], down_full, *scratch[8:10])
    query_plane = TwoLevelSum(False, *scratch[10:13], query_full, *scratch[13:15])
    pair_plane = TwoLevelSum(True, *scratch[15:18], pair_full, *scratch[18:20])
    out_plane = TwoLevelSum(True, *scratch[20:23], out_full, *scratch[23:25])

    def gather_of(i, src, dst):
        return Gather(src, dst, gather_sems.at[2 * i], gather_sems.at[2 * i + 1])

    greet(PlaneSum.peers() + SmallSum.peers())

    gather = gather_of(0, x, x_all)
    gather.start()
    across_z = PlaneSum.peer(1, 0)[1]
    pairs = (
        (qv_bias, qv_bias_two), (qkv, qkv_two), (out_weight, out_two),
        (up_bias, up_bias_two), (up, up_two), (down, down_two),
    )
    trades = [
        remote(mine, two.at[1], trade_sems.at[0], trade_sems.at[1], slot, across_z)
        for slot, (mine, two) in enumerate(pairs)
    ]
    for trade in trades:
        trade.start()
    for mine, two in pairs:
        two[0] = mine[...]
    numbers = segment_column(ids, column)

    def project(a, chip):
        rows = pl.ds(chip * CHIP, CHIP)
        product = dot_nt(chip_rows(x_all, chip), qkv_two[a].reshape(group, x.shape[1]))
        parts = [product[:, i * HEAD_DIM : (i + 1) * HEAD_DIM] for i in range(3)]
        queries[a, rows] = (parts[0] + qv_bias_two[a, 0:1]).astype(half)
        keys[a, rows] = parts[1].astype(half)
        values[a, rows] = (parts[2] + qv_bias_two[a, 1:2]).astype(half)

    @pl.loop(0, 4)
    def _(s):
        gather.ready(s)
        project(0, block_of(ring_order(s)) // 2)

    trades[0].wait_recv()
    trades[1].wait_recv()

    @pl.loop(0, 4)
    def _(chip):
        project(1, chip)

    trades[2].wait_recv()
    scatter = scatters[0]

    @pl.loop(0, 4)
    def _(i):
        k = ring_order(3 - i)
        chip = block_of(k) // 2
        rows = pl.ds(chip * CHIP, CHIP)
        allowed = column[rows, 0:1] == numbers
        for a in range(2):
            scores = dot_nt(queries[a, rows] * HEAD_DIM ** (-0.5), keys[a])
            masked = jnp.where(allowed, scores, MASKED)
            top = jnp.max(masked, axis=-1, keepdims=True)
            weights = jnp.exp(masked - top)
            mass = jnp.sum(weights, axis=-1, keepdims=True)
            lse[a, rows] = top + jnp.log(mass)
            probs = (weights * (1.0 / mass)).astype(half)
            context[rows, a * HEAD_DIM : (a + 1) * HEAD_DIM] = dot_nn(probs, values[a]).astype(half)
        put_term(scatter, chip, dot_nn(context[rows], flat_rows(out_two)))
        scatter.computed(k)

        @pl.when(i == 1)
        def _():
            scatter.across()

    scatter.sides()
    scatter.through()
    first = x[...].astype(wide) + scatter.result() + out_bias[...]
    normal, normed, inverse_one = layer_norm(first, gain1[...], bias1[...])
    own_rows[0] = normal.astype(half)

    gather = gather_of(1, own_rows.at[0], hidden_all)
    gather.start()
    hidden[...] = normal
    normed_one[...] = normed
    scatter = scatters[1]
    for trade in trades[3:]:
        trade.wait_recv()

    @pl.loop(0, 4)
    def _(s):
        @pl.when(s == 3)
        def _():
            scatter.sides()

        gather.ready(s)
        k = ring_order(s)
        chip = block_of(k) // 2
        rows = pl.ds(chip * CHIP, CHIP)
        for a in range(2):
            pre = dot_nn(chip_rows(hidden_all, chip), up_two[a]) + up_bias_two[a]
            value, gelu_slope = gelu_parts(pre)
            act[rows, a * shard : (a + 1) * shard] = value.astype(half)
            slope[rows, a * shard : (a + 1) * shard] = gelu_slope
        put_term(scatter, chip, dot_nn(act[rows], flat_rows(down_two)))
        scatter.computed(k)

    scatter.across()
    scatter.through()
    second = hidden[...] + scatter.result() + down_bias[...]
    output, normed_two, inverse_two = layer_norm(second, gain2[...], bias2[...])
    grad = cot[...].astype(wide)
    grad_second = norm_back(grad, normed_two, inverse_two, gain2[...])
    own_rows[1] = grad_second.astype(half)

    gather = gather_of(2, own_rows.at[1], d_second_all)
    gather.start()
    d_second[...] = grad_second
    out[...] = output.astype(half)
    vecs[pl.ds(3, 1)] = column_sum(grad_second)
    vecs[pl.ds(4, 1)] = column_sum(grad * normed_two)
    vecs[pl.ds(5, 1)] = column_sum(grad)
    vecs[pl.ds(6, 2)] = jnp.zeros((2, grad.shape[1]), wide)
    g_up_bias[...] = jnp.zeros_like(g_up_bias)
    scatter = scatters[2]

    @pl.loop(0, 4)
    def _(s):
        @pl.when(s == 3)
        def _():
            scatter.sides()

        gather.ready(s)
        k = ring_order(s)
        chip = block_of(k) // 2
        rows = pl.ds(chip * CHIP, CHIP)
        grad_pre = dot_nt(chip_rows(d_second_all, chip), flat_rows(down_two)) * slope[rows]
        g_up_bias[...] += column_sum(grad_pre)
        grad_pre = grad_pre.astype(half)
        d_pre[rows] = grad_pre
        put_term(scatter, chip, dot_nt(grad_pre[:, :shard], up_two[0]) + dot_nt(grad_pre[:, shard:], up_two[1]))
        scatter.computed(k)

    scatter.across()
    for a in range(2):
        part = dot_tn(act[:, a * shard : (a + 1) * shard], flat_rows(d_second_all)).astype(half)
        g_down[a] = part.reshape(PIECES, shard // PIECES, part.shape[1])
    down_plane.scatter(g_down)
    scatter.through()

    @pl.loop(0, 4)
    def _(i):
        columns = pl.ds(pl.multiple_of(i * 256, 256), 256)
        left = hidden_all[:, :, columns].reshape(RING * BLOCK, 256)
        part = dot_tn(left, d_pre[...]).astype(half)
        for a in range(2):
            g_up[a, pl.ds(2 * i, 2)] = part[:, a * shard : (a + 1) * shard].reshape(2, BLOCK, shard)

    d_hidden = d_second[...] + scatter.result()
    grad_first = norm_back(d_hidden, normed_one[...], inverse_one, gain1[...])
    own_rows[2] = grad_first.astype(half)

    gather = gather_of(3, own_rows.at[2], d_first_all)
    gather.start()
    up_plane.scatter(g_up)
    vecs[pl.ds(0, 1)] = column_sum(grad_first)
    vecs[pl.ds(1, 1)] = column_sum(d_hidden * normed_one[...])
    vecs[pl.ds(2, 1)] = column_sum(d_hidden)
    hidden[...] = grad_first
    small.start(vecs)
    d_keys[...] = jnp.zeros_like(d_keys)
    d_values[...] = jnp.zeros_like(d_values)
    query_sum[...] = jnp.zeros_like(query_sum)

    @pl.loop(0, 4)
    def _(s):
        @pl.when(s == 2)
        def _():
            down_plane.turn(g_down)

        gather.ready(s)

        @pl.when(s == 3)
        def _():
            up_plane.turn(g_up)

        chip = block_of(ring_order(s)) // 2
        rows = pl.ds(chip * CHIP, CHIP)
        d_context = dot_nt(chip_rows(d_first_all, chip), flat_rows(out_two)).astype(half)
        allowed = column[rows, 0:1] == numbers
        for a in range(2):
            d_head = d_context[:, a * HEAD_DIM : (a + 1) * HEAD_DIM]
            query = queries[a, rows]
            scores = dot_nt(query * HEAD_DIM ** (-0.5), keys[a])
            probs = jnp.exp(jnp.where(allowed, scores, MASKED) - lse[a, rows])
            d_values[a] += dot_tn(d_head, probs.astype(half))
            d_probs = dot_nt(d_head * HEAD_DIM ** (-0.5), values[a])
            mean = jnp.sum(probs * d_probs, axis=-1, keepdims=True)
            d_scores = (probs * (d_probs - mean)).astype(half)
            d_query = dot_nn(d_scores, keys[a])
            query_sum[a] += column_sum(d_query)
            d_qkv[rows, a * group : a * group + HEAD_DIM] = d_query.astype(half)
            d_keys[a] += dot_tn(query, d_scores)

    down_plane.share()
    shards = []
    for a in range(2):
        part = dot_tn(d_qkv[:, a * group : a * group + HEAD_DIM], flat_rows(x_all)).astype(half)
        g_query[a] = part.reshape(g_query.shape[1:])
    query_plane.scatter(g_query)
    for a in range(2):
        at = a * group + HEAD_DIM
        d_qkv[:, at : at + HEAD_DIM] = jnp.transpose(d_keys[a].astype(half))
        d_qkv[:, at + HEAD_DIM : at + 2 * HEAD_DIM] = jnp.transpose(d_values[a].astype(half))
        part = dot_tn(d_qkv[:, at : at + 2 * HEAD_DIM], flat_rows(x_all)).astype(half)
        g_pair[a] = part.reshape(g_pair.shape[1:])
        value_sum = jnp.sum(d_values[a], axis=1, keepdims=True)
        value_sum = jnp.transpose(jnp.broadcast_to(value_sum, (HEAD_DIM, 128)))[0:1]
        shards.append(
            jnp.concatenate(
                [
                    g_up_bias[:, a * shard : a * shard + 128],
                    g_up_bias[:, a * shard + 128 : (a + 1) * shard],
                    jnp.concatenate([query_sum[a], value_sum], axis=1),
                    jnp.zeros((5, 128), wide),
                ],
                axis=0,
            )
        )
    pair_plane.scatter(g_pair)
    part = dot_tn(context[...], flat_rows(d_first_all)).astype(half)
    for a in range(2):
        g_out[a] = part[a * HEAD_DIM : (a + 1) * HEAD_DIM].reshape(g_out.shape[1:])
    out_plane.scatter(g_out)
    small.plane(vecs, shards)
    scatter = scatters[3]

    @pl.loop(0, 4)
    def _(i):
        k = ring_order(3 - i)
        chip = block_of(k) // 2
        weight = qkv_two[...].reshape(2 * group, x.shape[1])
        put_term(scatter, chip, dot_nn(d_qkv[pl.ds(chip * CHIP, CHIP)], weight))
        scatter.computed(k)

        @pl.when(i == 1)
        def _():
            scatter.across()

    scatter.sides()
    up_plane.share()
    scatter.through()
    query_plane.turn(g_query)
    pair_plane.turn(g_pair)
    out_plane.turn(g_out)
    input_grad[...] = (hidden[...] + scatter.result()).astype(half)
    small.share(sums, shard_sums)
    late = (query_plane, pair_plane, out_plane)
    for plane in late:
        plane.share()
    for plane in (down_plane, up_plane, *late):
        plane.result()
    small.finish(sums)
    for i, (src, dst) in enumerate(((x, x_all), (x, hidden_all), (x, d_second_all), (x, d_first_all))):
        gather_of(i, src, dst).finish()
    for scatter in scatters:
        scatter.finish()
    for trade in trades:
        trade.wait_send()


def layer(x, ids, qkv, qv_bias, out_weight, out_bias, gain1, bias1, up, up_bias, down, down_bias, gain2, bias2, cot):
    rows, width = x.shape
    tokens = RING * rows
    shard = up.shape[1]
    one_head = (PIECES, HEAD_DIM // PIECES, width)
    two_heads = (PIECES, 2 * HEAD_DIM // PIECES, width)
    up_pieces = (PIECES, width // PIECES, shard)
    down_pieces = (PIECES, shard // PIECES, width)
    gathered = pltpu.VMEM((RING, rows, width), half)
    full_rows = pltpu.VMEM((rows, width), wide)
    head = pltpu.VMEM((2, tokens, HEAD_DIM), half)
    ff = pltpu.VMEM((tokens, 2 * shard), half)
    turned = pltpu.VMEM((2, HEAD_DIM, tokens), wide)
    scratch = [gathered] * 4 + [pltpu.VMEM((3, rows, width), half)] + [full_rows] * 3
    scratch += [head] * 3
    scratch += [
        pltpu.VMEM((2, tokens, 1), wide),
        pltpu.VMEM((tokens, 2 * HEAD_DIM), half),
        pltpu.VMEM((tokens, 128), jnp.int32),
    ]
    scratch += [pltpu.VMEM((2, *arr.shape), arr.dtype) for arr in (qkv, qv_bias, out_weight, up, up_bias, down)]
    scratch += [ff, pltpu.VMEM((tokens, 2 * shard), wide), ff]
    scratch += [pltpu.VMEM((2, *up_pieces), half), pltpu.VMEM((2, *down_pieces), half)]
    scratch += [pltpu.VMEM((1, 2 * shard), wide), pltpu.VMEM((8, width), wide)]
    scratch += [turned, turned, pltpu.VMEM((tokens, 6 * HEAD_DIM), half), pltpu.VMEM((2, 1, HEAD_DIM), wide)]
    scratch += [pltpu.VMEM((2, *pieces), half) for pieces in (one_head, two_heads, one_head)]
    scratch += [pltpu.SemaphoreType.DMA((8, Gather.slots)), pltpu.SemaphoreType.DMA((2, 6))]
    scratch += Scatter.scratch(width) * 4 + SmallSum.scratch
    for pieces in (up_pieces, down_pieces, one_head, two_heads, one_head):
        scratch += TwoLevelSum.scratch(*pieces[1:])
    return pl.pallas_call(
        layer_kernel,
        out_shape=(
            jax.ShapeDtypeStruct((rows, width), half),
            jax.ShapeDtypeStruct((rows, width), half),
            jax.ShapeDtypeStruct(up_pieces, half),
            jax.ShapeDtypeStruct(down_pieces, half),
            jax.ShapeDtypeStruct(one_head, half),
            jax.ShapeDtypeStruct(two_heads, half),
            jax.ShapeDtypeStruct(one_head, half),
            jax.ShapeDtypeStruct((8, width), wide),
            jax.ShapeDtypeStruct((8, 128), wide),
        ),
        in_specs=[VMEM_WHOLE] * 15,
        out_specs=(VMEM_WHOLE,) * 9,
        scratch_shapes=scratch,
        compiler_params=pltpu.CompilerParams(
            collective_id=0, has_side_effects=True, vmem_limit_bytes=VMEM_BYTES
        ),
    )(x, ids, qkv, qv_bias, out_weight, out_bias, gain1, bias1, up, up_bias, down, down_bias, gain2, bias2, cot)


def outputs_kernel(
    out_in, grad_in, up_full, down_full, query_full, pair_full, out_full, small, shard_sums,
    out, input_grad, g_qkv, g_qv_bias, g_out, g_out_bias, g_gain1, g_bias1, g_up, g_up_bias, g_down, g_down_bias,
    g_gain2, g_bias2,
):
    out[...] = out_in[...]
    input_grad[...] = grad_in[...]
    g_up[...] = flat_rows(up_full).astype(wide)
    g_down[...] = flat_rows(down_full).astype(wide)
    g_qkv[0] = flat_rows(query_full).astype(wide)
    g_qkv[1:] = flat_rows(pair_full).astype(wide).reshape(2, HEAD_DIM, out.shape[1])
    g_out[...] = flat_rows(out_full).astype(wide)
    for i, ref in enumerate((g_out_bias, g_gain1, g_bias1, g_down_bias, g_gain2, g_bias2)):
        ref[...] = small[pl.ds(i, 1)]
    for i in range(2):
        g_up_bias[:, i * 128 : (i + 1) * 128] = shard_sums[pl.ds(i, 1)]
        g_qv_bias[pl.ds(i, 1)] = shard_sums[pl.ds(2, 1), i * HEAD_DIM : (i + 1) * HEAD_DIM]


def write_outputs(results):
    rows, width = results[0].shape
    ff = results[2].shape[2]
    vector = jax.ShapeDtypeStruct((1, width), wide)
    block = jax.ShapeDtypeStruct((rows, width), half)
    return pl.pallas_call(
        outputs_kernel,
        out_shape=(
            block,
            block,
            jax.ShapeDtypeStruct((3, HEAD_DIM, width), wide),
            jax.ShapeDtypeStruct((2, HEAD_DIM), wide),
            jax.ShapeDtypeStruct((HEAD_DIM, width), wide),
            vector,
            vector,
            vector,
            jax.ShapeDtypeStruct((width, ff), wide),
            jax.ShapeDtypeStruct((1, ff), wide),
            jax.ShapeDtypeStruct((ff, width), wide),
            vector,
            vector,
            vector,
        ),
        in_specs=[VMEM_WHOLE] * 9,
        out_specs=(VMEM_WHOLE,) * 14,
    )(*results)


def row(vector):
    return vector.reshape(1, vector.shape[0])


def per_device(
    block_input,
    segment_ids,
    qkv_weight,
    qv_bias,
    out_weight,
    out_bias,
    norm1_gain,
    norm1_bias,
    up_weight,
    up_bias,
    down_weight,
    down_bias,
    norm2_gain,
    norm2_bias,
    cotangent,
):
    results = layer(
        block_input, segment_ids, jnp.swapaxes(qkv_weight, 1, 2), qv_bias, out_weight, row(out_bias),
        row(norm1_gain), row(norm1_bias), up_weight, row(up_bias), down_weight, row(down_bias),
        row(norm2_gain), row(norm2_bias), cotangent,
    )
    out, input_grad, g_qkv, g_qv_bias, g_out, *vectors = write_outputs(results)
    g_out_bias, g_gain1, g_bias1, g_up, g_up_bias, g_down, g_down_bias, g_gain2, g_bias2 = (
        arr.reshape(-1) if arr.shape[0] == 1 else arr for arr in vectors
    )
    return (
        out, input_grad, jnp.swapaxes(g_qkv, 1, 2), g_qv_bias, g_out, g_out_bias, g_gain1, g_bias1,
        g_up, g_up_bias, g_down, g_down_bias, g_gain2, g_bias2,
    )


def solution(mesh):
    placed = (
        P(("dp", "tensor"), None),
        P("dp", None),
        P(None, None, "tensor"),
        P(None, "tensor"),
        P("tensor", None),
        P(),
        P(),
        P(),
        P(None, "tensor"),
        P("tensor"),
        P("tensor", None),
        P(),
        P(),
        P(),
        P(("dp", "tensor"), None),
    )
    return jax.shard_map(
        per_device,
        mesh=mesh,
        in_specs=placed,
        out_specs=(
            P(("dp", "tensor"), None),
            P(("dp", "tensor"), None),
            P(None, None, "tensor"),
            P(None, "tensor"),
            P("tensor", None),
            P(),
            P(),
            P(),
            P(None, "tensor"),
            P("tensor"),
            P("tensor", None),
            P(),
            P(),
            P(),
        ),
        check_vma=False,
    )
```

```python
import jax
import jax.numpy as jnp
from jax import lax
from jax.experimental import pallas as pl
from jax.experimental.pallas import tpu as pltpu
from jax.sharding import PartitionSpec as P

HEAD_DIM = 64
RING = 8
BLOCK = 128
HALF = 64
CHIP = 2 * BLOCK
PIECES = 8
MESH = pl.DeviceIdType.MESH
VMEM_WHOLE = pl.BlockSpec(memory_space=pltpu.VMEM)
VMEM_BYTES = 60 * 1024 * 1024
half = jnp.bfloat16
wide = jnp.float32


EPS = 1e-12
MASKED = -1e30
ROOT_HALF = 0.7071067811865476
INV_ROOT_TAU = 0.3989422804014327


def ring_place():
    t = lax.axis_index("tensor")
    dp = lax.axis_index("dp")
    base = (t // RING) * RING
    j = t % RING
    x = j // 2
    c = j % 2

    def block_of(step, other=False):
        xx = lax.rem(x + step + 4, 4)
        return xx * 2 + ((1 - c) if other else c)

    def device_of(step, other=False):
        return (dp, base + block_of(step, other))

    return block_of, device_of


def ring_order(s):
    return s + s // 2 - 2 * (s // 3)


def greet(devices):
    barrier = pltpu.get_barrier_semaphore()
    for device in devices:
        pl.semaphore_signal(barrier, inc=1, device_id=device, device_id_type=MESH)
    pl.semaphore_wait(barrier, len(devices))


def greet_ring():
    _, device_of = ring_place()
    greet((device_of(1), device_of(-1), device_of(0, True)))


def remote(src, dst, send, recv, slot, device):
    return pltpu.make_async_remote_copy(
        src_ref=src,
        dst_ref=dst,
        send_sem=send.at[slot],
        recv_sem=recv.at[slot],
        device_id=device,
        device_id_type=MESH,
    )


FIRST = pl.ds(0, HALF)
SECOND = pl.ds(HALF, HALF)


class Gather:
    slots = 13

    def __init__(self, src, out, send, recv):
        self.src, self.out, self.send, self.recv = src, out, send, recv
        self.block_of, self.device_of = ring_place()
        self.partner = self.device_of(0, True)

    def copy(self, place, slot, device):
        return remote(place, place, self.send, self.recv, slot, device)

    def start(self):
        src, at = self.src, self.out.at
        mine, right, left = self.block_of(0), self.device_of(1), self.device_of(-1)
        for part, slot, device in ((FIRST, 0, right), (SECOND, 3, left), (SECOND, 1, right), (FIRST, 2, left)):
            remote(src.at[part], at[mine, part], self.send, self.recv, slot, device).start()
        remote(src, at[mine], self.send, self.recv, 6, self.partner).start()
        self.out[pl.ds(mine, 1)] = src[...].reshape(1, *src.shape)

    def pass_on(self, slot, step, part, share_slot, device=None, device_slot=None):
        place = self.out.at[self.block_of(step), part]
        self.copy(place, slot, self.partner).wait_recv()
        if device is not None:
            self.copy(place, device_slot, device).start()
        self.copy(place, share_slot, self.partner).start()

    def shared(self, step, slots):
        for slot, part in zip(slots, (FIRST, SECOND)):
            self.copy(self.out.at[self.block_of(step, True), part], slot, self.partner).wait_recv()

    def ready(self, s):
        @pl.when(s == 0)
        def _():
            self.copy(self.out.at[self.block_of(0, True)], 6, self.partner).wait_recv()

        @pl.when(s == 1)
        def _():
            self.pass_on(0, -1, FIRST, 7, self.device_of(1), 4)
            self.pass_on(3, 1, SECOND, 10, self.device_of(-1), 5)
            self.pass_on(2, 1, FIRST, 9)
            self.pass_on(1, -1, SECOND, 8)
            self.shared(1, (9, 10))

        @pl.when(s == 2)
        def _():
            self.shared(-1, (7, 8))

        @pl.when(s == 3)
        def _():
            self.pass_on(4, 2, FIRST, 11)
            self.pass_on(5, 2, SECOND, 12)
            self.shared(2, (11, 12))

    def finish(self):
        half_place = self.out.at[0, FIRST]
        for slot in range(13):
            self.copy(self.out.at[0] if slot == 6 else half_place, slot, self.partner).wait_send()


class Scatter:
    slots = 10

    @staticmethod
    def scratch(width):
        return [
            pltpu.VMEM((RING, BLOCK, width), half),
            pltpu.VMEM((4, BLOCK, width), half),
            pltpu.VMEM((6, HALF, width), half),
            pltpu.VMEM((2, HALF, width), half),
            pltpu.VMEM((2, 2, HALF, width), half),
            pltpu.SemaphoreType.DMA((10,)),
            pltpu.SemaphoreType.DMA((10,)),
        ]

    def __init__(self, y, pair, stage, transit, final, send, recv):
        self.y, self.pair, self.stage, self.transit, self.final = y, pair, stage, transit, final
        self.send, self.recv = send, recv
        self.block_of, self.device_of = ring_place()
        self.partner = self.device_of(0, True)

    def computed(self, k):
        remote(self.y.at[self.block_of(k, True)], self.pair.at[k], self.send, self.recv, k, self.partner).start()

    def arrived(self, place, slot):
        remote(place, place, self.send, self.recv, slot, self.partner).wait_recv()

    def chip_sum(self, k, part):
        return self.y[self.block_of(k), part].astype(wide) + self.pair[k, part].astype(wide)

    def forward(self, at, value, place, slot, device):
        self.stage[at] = value.astype(half)
        remote(self.stage.at[at], place, self.send, self.recv, slot, device).start()

    def sides(self):
        self.arrived(self.pair.at[1], 1)
        self.forward(2, self.chip_sum(1, SECOND), self.final.at[0, 1], 6, self.device_of(1))
        self.arrived(self.pair.at[3], 3)
        self.forward(3, self.chip_sum(3, FIRST), self.final.at[1, 0], 7, self.device_of(-1))

    def across(self):
        self.arrived(self.pair.at[2], 2)
        self.forward(0, self.chip_sum(2, FIRST), self.transit.at[0], 4, self.device_of(1))
        self.forward(1, self.chip_sum(2, SECOND), self.transit.at[1], 5, self.device_of(-1))

    def through(self):
        self.arrived(self.transit.at[0], 4)
        value = self.chip_sum(1, FIRST) + self.transit[0].astype(wide)
        self.forward(4, value, self.final.at[0, 0], 8, self.device_of(1))
        self.arrived(self.transit.at[1], 5)
        value = self.chip_sum(3, SECOND) + self.transit[1].astype(wide)
        self.forward(5, value, self.final.at[1, 1], 9, self.device_of(-1))

    def result(self):
        self.arrived(self.pair.at[0], 0)
        for slot, place in ((6, (0, 1)), (7, (1, 0)), (8, (0, 0)), (9, (1, 1))):
            self.arrived(self.final.at[place], slot)
        final = self.final
        rows = [
            self.chip_sum(0, part) + final[0, h].astype(wide) + final[1, h].astype(wide)
            for h, part in enumerate((FIRST, SECOND))
        ]
        return jnp.concatenate(rows, axis=0)

    def finish(self):
        for slot in range(10):
            place = self.pair.at[0] if slot < 4 else self.transit.at[0]
            remote(place, place, self.send, self.recv, slot, self.partner).wait_send()


def dot_nn(left, right):
    return lax.dot_general(left, right, (((1,), (0,)), ((), ())), preferred_element_type=wide)


def dot_nt(left, right):
    return lax.dot_general(left, right, (((1,), (1,)), ((), ())), preferred_element_type=wide)


def dot_tn(left, right):
    return lax.dot_general(left, right, (((0,), (0,)), ((), ())), preferred_element_type=wide)


def layer_norm(rows, gain, shift):
    center = rows - jnp.mean(rows, axis=-1, keepdims=True)
    inverse = lax.rsqrt(jnp.mean(center * center, axis=-1, keepdims=True) + EPS)
    normed = center * inverse
    return (normed * gain + shift, normed, inverse)


def norm_back(grad, normed, inverse, gain):
    scaled = grad * gain
    return inverse * (
        scaled
        - jnp.mean(scaled, axis=-1, keepdims=True)
        - normed * jnp.mean(scaled * normed, axis=-1, keepdims=True)
    )


def gelu_parts(pre):
    cumul = 0.5 * (1.0 + lax.erf(pre * ROOT_HALF))
    return (pre * cumul, cumul + pre * jnp.exp(-0.5 * pre * pre) * INV_ROOT_TAU)


def column_sum(rows):
    return jnp.sum(rows, axis=0, keepdims=True)


def chip_rows(ref, chip):
    block = ref[pl.ds(2 * chip, 2)]
    return block.reshape(CHIP, block.shape[2])


def flat_rows(ref):
    block = ref[...]
    return block.reshape(block.shape[0] * block.shape[1], block.shape[2])


class PlaneSum:
    def __init__(self, land, full, send, recv):
        self.land, self.full, self.send, self.recv = land, full, send, recv
        t, dp = lax.axis_index("tensor"), lax.axis_index("dp")
        self.t, self.dp = t, dp

    @staticmethod
    def peer(a, r):
        t, dp = lax.axis_index("tensor"), lax.axis_index("dp")
        other = lax.rem(dp // 4 + r // 4, 2) * 4 + lax.rem(dp + r, 4)
        return other, (other, lax.rem(t + a * RING, 2 * RING))

    @staticmethod
    def peers():
        return [PlaneSum.peer(n // PIECES, n % PIECES)[1] for n in range(1, 2 * PIECES)]

    def hand_out(self, total):
        self.full[pl.ds(self.dp, 1)] = total.astype(half).reshape(1, *total.shape)
        self.send_piece(self.dp, 15, lax.rem(self.dp + 4, PIECES))
        for r in range(1, 4):
            self.send_piece(self.dp, 15 + r, self.along_y(r))

    def send_piece(self, piece, slot, other):
        place = self.full.at[piece]
        remote(place, place, self.send, self.recv, slot, (other, self.t)).start()

    def along_y(self, r):
        return (self.dp // 4) * 4 + lax.rem(self.dp + r, 4)

    def got(self, piece, slot):
        place = self.full.at[piece]
        remote(place, place, self.send, self.recv, slot, (self.dp, self.t)).wait_recv()

    def pass_along(self):
        neighbour = lax.rem(self.dp + 4, PIECES)
        self.got(neighbour, 15)
        for r in range(1, 4):
            self.send_piece(neighbour, 18 + r, self.along_y(r))

    def result(self):
        for r in range(1, 4):
            self.got(self.along_y(4 - r), 15 + r)
            self.got(lax.rem(self.along_y(4 - r) + 4, PIECES), 18 + r)
        self.sent()


class TwoLevelSum(PlaneSum):
    def __init__(self, z_first, near, mid, far, full, send, recv):
        super().__init__(far, full, send, recv)
        self.z_first, self.near, self.mid = z_first, near, mid

    @staticmethod
    def peer_z(n):
        dp, t = lax.axis_index("dp"), lax.axis_index("tensor")
        z_lo = lax.rem(dp // 4 + n % 2, 2)
        return z_lo, (z_lo * 4 + lax.rem(dp, 4), lax.rem(t + (n // 2) * RING, 2 * RING))

    @staticmethod
    def peer_y(r):
        dp, t = lax.axis_index("dp"), lax.axis_index("tensor")
        y = lax.rem(dp + r, 4)
        return y, ((dp // 4) * 4 + y, t)

    def here(self):
        return (self.dp, self.t)

    def scatter(self, grads):
        for n in range(1, 4):
            if self.z_first:
                z_lo, device = self.peer_z(n)
                remote(grads.at[n // 2, pl.ds(4 * z_lo, 4)], self.near.at[n - 1], self.send, self.recv, n - 1, device).start()
            else:
                y, device = self.peer_y(n)
                for m in range(4):
                    source = grads.at[m // 2, 4 * (m % 2) + y]
                    remote(source, self.near.at[n - 1, m], self.send, self.recv, 4 * (n - 1) + m, device).start()

    def turn(self, grads):
        count = 3 if self.z_first else 12
        for slot in range(count):
            place = self.near.at[slot] if self.z_first else self.near.at[slot // 4, slot % 4]
            remote(place, place, self.send, self.recv, slot, self.here()).wait_recv()
        y, z_lo = lax.rem(self.dp, 4), self.dp // 4
        for m in range(4):
            mine = grads[0, 4 * z_lo + m] if self.z_first else grads[m // 2, 4 * (m % 2) + y]
            total = mine.astype(wide)
            for n in range(3):
                total += self.near[n, m].astype(wide)
            self.mid[m] = total.astype(half)
        for n in range(1, 4):
            if self.z_first:
                at, device = self.peer_y(n)
            else:
                z_lo_there, device = self.peer_z(n)
                at = 2 * (n // 2) + z_lo_there
            remote(self.mid.at[at], self.land.at[n - 1], self.send, self.recv, 11 + n, device).start()

    def share(self):
        at = lax.rem(self.dp, 4) if self.z_first else self.dp // 4
        total = self.mid[at].astype(wide)
        for n in range(3):
            place = self.land.at[n]
            remote(place, place, self.send, self.recv, 12 + n, self.here()).wait_recv()
            total += self.land[n].astype(wide)
        self.hand_out(total)

    def sent(self):
        for slot in range(3 if self.z_first else 12):
            place = self.near.at[0] if self.z_first else self.near.at[0, 0]
            remote(place, place, self.send, self.recv, slot, self.here()).wait_send()
        for slot in range(12, 22):
            place = self.land.at[0]
            remote(place, place, self.send, self.recv, slot, self.here()).wait_send()

    @staticmethod
    def scratch(rows, width):
        return [
            pltpu.VMEM((3, 4, rows, width), half),
            pltpu.VMEM((4, rows, width), half),
            pltpu.VMEM((3, rows, width), half),
            pltpu.SemaphoreType.DMA((22,)),
            pltpu.SemaphoreType.DMA((22,)),
        ]


class SmallSum:
    scratch = [
        pltpu.VMEM((RING, 8, 128), wide),
        pltpu.VMEM((2, 16, 128), wide),
        pltpu.VMEM((15, 16, 128), wide),
        pltpu.SemaphoreType.DMA((29,)),
        pltpu.SemaphoreType.DMA((29,)),
    ]

    def __init__(self, line, base, land, send, recv):
        self.line, self.base, self.land, self.send, self.recv = line, base, land, send, recv
        self.t, self.dp = lax.axis_index("tensor"), lax.axis_index("dp")

    @staticmethod
    def line_peer(r):
        t, dp = lax.axis_index("tensor"), lax.axis_index("dp")
        return (dp, (t // RING) * RING + lax.rem(t + r, RING))

    @staticmethod
    def peers():
        return [SmallSum.line_peer(r) for r in range(1, RING)]

    def slab(self, ref, r):
        return ref.at[:, pl.ds(pl.multiple_of(lax.rem(self.t + r, RING) * 128, 128), 128)]

    def arrived(self, place, slot):
        remote(place, place, self.send, self.recv, slot, (self.dp, self.t)).wait_recv()

    def start(self, vecs):
        for r in range(1, RING):
            remote(self.slab(vecs, r), self.line.at[r], self.send, self.recv, 14 + r, self.line_peer(r)).start()

    def plane(self, vecs, shards):
        total = self.slab(vecs, 0)[...]
        for r in range(1, RING):
            self.arrived(self.line.at[r], 14 + r)
            total += self.line[r]
        for a in range(2):
            self.base[a, 0:8] = total
            self.base[a, 8:16] = shards[a]
        for n in range(1, 2 * PIECES):
            _, device = PlaneSum.peer(n // PIECES, n % PIECES)
            remote(self.base.at[n // PIECES], self.land.at[n - 1], self.send, self.recv, n - 1, device).start()

    def share(self, sums, shard_sums):
        total = self.base[0]
        for n in range(15):
            self.arrived(self.land.at[n], n)
            total += self.land[n]
        mine = self.slab(sums, 0)
        mine[...] = total[0:8]
        shard_sums[...] = total[8:16]
        for r in range(1, RING):
            remote(mine, mine, self.send, self.recv, 21 + r, self.line_peer(r)).start()

    def finish(self, sums):
        for r in range(1, RING):
            self.arrived(self.slab(sums, RING - r), 21 + r)
        for slot in range(29):
            place = self.land.at[0] if slot < 15 else self.line.at[0]
            remote(place, place, self.send, self.recv, slot, (self.dp, self.t)).wait_send()


def segment_column(ids, column):
    upper = lax.axis_index("tensor") // RING
    numbers = jnp.where(upper == 0, ids[pl.ds(0, 1)], ids[pl.ds(1, 1)])
    column[...] = jnp.transpose(jnp.broadcast_to(numbers, (128, numbers.shape[1])))
    return numbers


def put_term(scatter, chip, term):
    scatter.y[pl.ds(2 * chip, 2)] = term.astype(half).reshape(2, BLOCK, term.shape[1])


def layer_kernel(
    x, ids, qkv, qv_bias, out_weight, out_bias, gain1, bias1, up, up_bias, down, down_bias, gain2, bias2, cot,
    out, input_grad, up_full, down_full, query_full, pair_full, out_full, sums, shard_sums,
    x_all, hidden_all, d_second_all, d_first_all, own_rows, hidden, normed_one, d_second,
    queries, keys, values, lse, context, column,
    qkv_two, qv_bias_two, out_two, up_two, up_bias_two, down_two,
    act, slope, d_pre, g_up, g_down, g_up_bias, vecs,
    d_keys, d_values, d_qkv, query_sum, g_query, g_pair, g_out,
    gather_sems, trade_sems, *scratch,
):
    block_of, device_of = ring_place()
    shard = up.shape[1]
    group = 3 * HEAD_DIM
    scatters = [Scatter(*scratch[7 * i : 7 * i + 7]) for i in range(4)]
    scratch = scratch[28:]
    small, scratch = SmallSum(*scratch[:5]), scratch[5:]
    up_plane = TwoLevelSum(False, *scratch[0:3], up_full, *scratch[3:5])
    down_plane = TwoLevelSum(True, *scratch[5:8], down_full, *scratch[8:10])
    query_plane = TwoLevelSum(False, *scratch[10:13], query_full, *scratch[13:15])
    pair_plane = TwoLevelSum(True, *scratch[15:18], pair_full, *scratch[18:20])
    out_plane = TwoLevelSum(True, *scratch[20:23], out_full, *scratch[23:25])

    def gather_of(i, src, dst):
        return Gather(src, dst, gather_sems.at[2 * i], gather_sems.at[2 * i + 1])

    greet(PlaneSum.peers() + SmallSum.peers())

    gather = gather_of(0, x, x_all)
    gather.start()
    across_z = PlaneSum.peer(1, 0)[1]
    pairs = (
        (qv_bias, qv_bias_two), (qkv, qkv_two), (out_weight, out_two),
        (up_bias, up_bias_two), (up, up_two), (down, down_two),
    )
    trades = [
        remote(mine, two.at[1], trade_sems.at[0], trade_sems.at[1], slot, across_z)
        for slot, (mine, two) in enumerate(pairs)
    ]
    for trade in trades:
        trade.start()
    for mine, two in pairs:
        two[0] = mine[...]
    numbers = segment_column(ids, column)

    def project(a, chip):
        rows = pl.ds(chip * CHIP, CHIP)
        product = dot_nt(chip_rows(x_all, chip), qkv_two[a].reshape(group, x.shape[1]))
        parts = [product[:, i * HEAD_DIM : (i + 1) * HEAD_DIM] for i in range(3)]
        queries[a, rows] = (parts[0] + qv_bias_two[a, 0:1]).astype(half)
        keys[a, rows] = parts[1].astype(half)
        values[a, rows] = (parts[2] + qv_bias_two[a, 1:2]).astype(half)

    @pl.loop(0, 4)
    def _(s):
        gather.ready(s)
        project(0, block_of(ring_order(s)) // 2)

    trades[0].wait_recv()
    trades[1].wait_recv()

    @pl.loop(0, 4)
    def _(chip):
        project(1, chip)

    trades[2].wait_recv()
    scatter = scatters[0]

    @pl.loop(0, 4)
    def _(i):
        k = ring_order(3 - i)
        chip = block_of(k) // 2
        rows = pl.ds(chip * CHIP, CHIP)
        allowed = column[rows, 0:1] == numbers
        for a in range(2):
            scores = dot_nt(queries[a, rows] * HEAD_DIM ** (-0.5), keys[a])
            masked = jnp.where(allowed, scores, MASKED)
            top = jnp.max(masked, axis=-1, keepdims=True)
            weights = jnp.exp(masked - top)
            mass = jnp.sum(weights, axis=-1, keepdims=True)
            lse[a, rows] = top + jnp.log(mass)
            probs = (weights * (1.0 / mass)).astype(half)
            context[rows, a * HEAD_DIM : (a + 1) * HEAD_DIM] = dot_nn(probs, values[a]).astype(half)
        put_term(scatter, chip, dot_nn(context[rows], flat_rows(out_two)))
        scatter.computed(k)

        @pl.when(i == 1)
        def _():
            scatter.across()

    scatter.sides()
    scatter.through()
    first = x[...].astype(wide) + scatter.result() + out_bias[...]
    normal, normed, inverse_one = layer_norm(first, gain1[...], bias1[...])
    own_rows[0] = normal.astype(half)

    gather = gather_of(1, own_rows.at[0], hidden_all)
    gather.start()
    hidden[...] = normal
    normed_one[...] = normed
    scatter = scatters[1]
    for trade in trades[3:]:
        trade.wait_recv()

    @pl.loop(0, 4)
    def _(s):
        @pl.when(s == 3)
        def _():
            scatter.sides()

        gather.ready(s)
        k = ring_order(s)
        chip = block_of(k) // 2
        rows = pl.ds(chip * CHIP, CHIP)
        for a in range(2):
            pre = dot_nn(chip_rows(hidden_all, chip), up_two[a]) + up_bias_two[a]
            value, gelu_slope = gelu_parts(pre)
            act[rows, a * shard : (a + 1) * shard] = value.astype(half)
            slope[rows, a * shard : (a + 1) * shard] = gelu_slope
        put_term(scatter, chip, dot_nn(act[rows], flat_rows(down_two)))
        scatter.computed(k)

    scatter.across()
    scatter.through()
    second = hidden[...] + scatter.result() + down_bias[...]
    output, normed_two, inverse_two = layer_norm(second, gain2[...], bias2[...])
    grad = cot[...].astype(wide)
    grad_second = norm_back(grad, normed_two, inverse_two, gain2[...])
    own_rows[1] = grad_second.astype(half)

    gather = gather_of(2, own_rows.at[1], d_second_all)
    gather.start()
    d_second[...] = grad_second
    out[...] = output.astype(half)
    vecs[pl.ds(3, 1)] = column_sum(grad_second)
    vecs[pl.ds(4, 1)] = column_sum(grad * normed_two)
    vecs[pl.ds(5, 1)] = column_sum(grad)
    vecs[pl.ds(6, 2)] = jnp.zeros((2, grad.shape[1]), wide)
    g_up_bias[...] = jnp.zeros_like(g_up_bias)
    scatter = scatters[2]

    @pl.loop(0, 4)
    def _(s):
        @pl.when(s == 3)
        def _():
            scatter.sides()

        gather.ready(s)
        k = ring_order(s)
        chip = block_of(k) // 2
        rows = pl.ds(chip * CHIP, CHIP)
        grad_pre = dot_nt(chip_rows(d_second_all, chip), flat_rows(down_two)) * slope[rows]
        g_up_bias[...] += column_sum(grad_pre)
        grad_pre = grad_pre.astype(half)
        d_pre[rows] = grad_pre
        put_term(scatter, chip, dot_nt(grad_pre[:, :shard], up_two[0]) + dot_nt(grad_pre[:, shard:], up_two[1]))
        scatter.computed(k)

    scatter.across()
    for a in range(2):
        part = dot_tn(act[:, a * shard : (a + 1) * shard], flat_rows(d_second_all)).astype(half)
        g_down[a] = part.reshape(PIECES, shard // PIECES, part.shape[1])
    down_plane.scatter(g_down)
    scatter.through()

    @pl.loop(0, 4)
    def _(i):
        columns = pl.ds(pl.multiple_of(i * 256, 256), 256)
        left = hidden_all[:, :, columns].reshape(RING * BLOCK, 256)
        part = dot_tn(left, d_pre[...]).astype(half)
        for a in range(2):
            g_up[a, pl.ds(2 * i, 2)] = part[:, a * shard : (a + 1) * shard].reshape(2, BLOCK, shard)

    d_hidden = d_second[...] + scatter.result()
    grad_first = norm_back(d_hidden, normed_one[...], inverse_one, gain1[...])
    own_rows[2] = grad_first.astype(half)

    gather = gather_of(3, own_rows.at[2], d_first_all)
    gather.start()
    up_plane.scatter(g_up)
    vecs[pl.ds(0, 1)] = column_sum(grad_first)
    vecs[pl.ds(1, 1)] = column_sum(d_hidden * normed_one[...])
    vecs[pl.ds(2, 1)] = column_sum(d_hidden)
    hidden[...] = grad_first
    small.start(vecs)
    d_keys[...] = jnp.zeros_like(d_keys)
    d_values[...] = jnp.zeros_like(d_values)
    query_sum[...] = jnp.zeros_like(query_sum)

    @pl.loop(0, 4)
    def _(s):
        @pl.when(s == 2)
        def _():
            down_plane.turn(g_down)

        gather.ready(s)

        @pl.when(s == 3)
        def _():
            up_plane.turn(g_up)

        chip = block_of(ring_order(s)) // 2
        rows = pl.ds(chip * CHIP, CHIP)
        d_context = dot_nt(chip_rows(d_first_all, chip), flat_rows(out_two)).astype(half)
        allowed = column[rows, 0:1] == numbers
        for a in range(2):
            d_head = d_context[:, a * HEAD_DIM : (a + 1) * HEAD_DIM]
            query = queries[a, rows]
            scores = dot_nt(query * HEAD_DIM ** (-0.5), keys[a])
            probs = jnp.exp(jnp.where(allowed, scores, MASKED) - lse[a, rows])
            d_values[a] += dot_tn(d_head, probs.astype(half))
            d_probs = dot_nt(d_head * HEAD_DIM ** (-0.5), values[a])
            mean = jnp.sum(probs * d_probs, axis=-1, keepdims=True)
            d_scores = (probs * (d_probs - mean)).astype(half)
            d_query = dot_nn(d_scores, keys[a])
            query_sum[a] += column_sum(d_query)
            d_qkv[rows, a * group : a * group + HEAD_DIM] = d_query.astype(half)
            d_keys[a] += dot_tn(query, d_scores)

    down_plane.share()
    shards = []
    for a in range(2):
        part = dot_tn(d_qkv[:, a * group : a * group + HEAD_DIM], flat_rows(x_all)).astype(half)
        g_query[a] = part.reshape(g_query.shape[1:])
    query_plane.scatter(g_query)
    for a in range(2):
        at = a * group + HEAD_DIM
        d_qkv[:, at : at + HEAD_DIM] = jnp.transpose(d_keys[a].astype(half))
        d_qkv[:, at + HEAD_DIM : at + 2 * HEAD_DIM] = jnp.transpose(d_values[a].astype(half))
        part = dot_tn(d_qkv[:, at : at + 2 * HEAD_DIM], flat_rows(x_all)).astype(half)
        g_pair[a] = part.reshape(g_pair.shape[1:])
        value_sum = jnp.sum(d_values[a], axis=1, keepdims=True)
        value_sum = jnp.transpose(jnp.broadcast_to(value_sum, (HEAD_DIM, 128)))[0:1]
        shards.append(
            jnp.concatenate(
                [
                    g_up_bias[:, a * shard : a * shard + 128],
                    g_up_bias[:, a * shard + 128 : (a + 1) * shard],
                    jnp.concatenate([query_sum[a], value_sum], axis=1),
                    jnp.zeros((5, 128), wide),
                ],
                axis=0,
            )
        )
    pair_plane.scatter(g_pair)
    part = dot_tn(context[...], flat_rows(d_first_all)).astype(half)
    for a in range(2):
        g_out[a] = part[a * HEAD_DIM : (a + 1) * HEAD_DIM].reshape(g_out.shape[1:])
    out_plane.scatter(g_out)
    small.plane(vecs, shards)
    down_plane.pass_along()
    scatter = scatters[3]

    @pl.loop(0, 4)
    def _(i):
        k = ring_order(3 - i)
        chip = block_of(k) // 2
        weight = qkv_two[...].reshape(2 * group, x.shape[1])
        put_term(scatter, chip, dot_nn(d_qkv[pl.ds(chip * CHIP, CHIP)], weight))
        scatter.computed(k)

        @pl.when(i == 1)
        def _():
            scatter.across()

    scatter.sides()
    up_plane.share()
    scatter.through()
    up_plane.pass_along()
    query_plane.turn(g_query)
    pair_plane.turn(g_pair)
    out_plane.turn(g_out)
    input_grad[...] = (hidden[...] + scatter.result()).astype(half)
    small.share(sums, shard_sums)
    late = (query_plane, pair_plane, out_plane)
    for plane in late:
        plane.share()
    for plane in late:
        plane.pass_along()
    for plane in (down_plane, up_plane, *late):
        plane.result()
    small.finish(sums)
    for i, (src, dst) in enumerate(((x, x_all), (x, hidden_all), (x, d_second_all), (x, d_first_all))):
        gather_of(i, src, dst).finish()
    for scatter in scatters:
        scatter.finish()
    for trade in trades:
        trade.wait_send()


def layer(x, ids, qkv, qv_bias, out_weight, out_bias, gain1, bias1, up, up_bias, down, down_bias, gain2, bias2, cot):
    rows, width = x.shape
    tokens = RING * rows
    shard = up.shape[1]
    one_head = (PIECES, HEAD_DIM // PIECES, width)
    two_heads = (PIECES, 2 * HEAD_DIM // PIECES, width)
    up_pieces = (PIECES, width // PIECES, shard)
    down_pieces = (PIECES, shard // PIECES, width)
    gathered = pltpu.VMEM((RING, rows, width), half)
    full_rows = pltpu.VMEM((rows, width), wide)
    head = pltpu.VMEM((2, tokens, HEAD_DIM), half)
    ff = pltpu.VMEM((tokens, 2 * shard), half)
    turned = pltpu.VMEM((2, HEAD_DIM, tokens), wide)
    scratch = [gathered] * 4 + [pltpu.VMEM((3, rows, width), half)] + [full_rows] * 3
    scratch += [head] * 3
    scratch += [
        pltpu.VMEM((2, tokens, 1), wide),
        pltpu.VMEM((tokens, 2 * HEAD_DIM), half),
        pltpu.VMEM((tokens, 128), jnp.int32),
    ]
    scratch += [pltpu.VMEM((2, *arr.shape), arr.dtype) for arr in (qkv, qv_bias, out_weight, up, up_bias, down)]
    scratch += [ff, pltpu.VMEM((tokens, 2 * shard), wide), ff]
    scratch += [pltpu.VMEM((2, *up_pieces), half), pltpu.VMEM((2, *down_pieces), half)]
    scratch += [pltpu.VMEM((1, 2 * shard), wide), pltpu.VMEM((8, width), wide)]
    scratch += [turned, turned, pltpu.VMEM((tokens, 6 * HEAD_DIM), half), pltpu.VMEM((2, 1, HEAD_DIM), wide)]
    scratch += [pltpu.VMEM((2, *pieces), half) for pieces in (one_head, two_heads, one_head)]
    scratch += [pltpu.SemaphoreType.DMA((8, Gather.slots)), pltpu.SemaphoreType.DMA((2, 6))]
    scratch += Scatter.scratch(width) * 4 + SmallSum.scratch
    for pieces in (up_pieces, down_pieces, one_head, two_heads, one_head):
        scratch += TwoLevelSum.scratch(*pieces[1:])
    return pl.pallas_call(
        layer_kernel,
        out_shape=(
            jax.ShapeDtypeStruct((rows, width), half),
            jax.ShapeDtypeStruct((rows, width), half),
            jax.ShapeDtypeStruct(up_pieces, half),
            jax.ShapeDtypeStruct(down_pieces, half),
            jax.ShapeDtypeStruct(one_head, half),
            jax.ShapeDtypeStruct(two_heads, half),
            jax.ShapeDtypeStruct(one_head, half),
            jax.ShapeDtypeStruct((8, width), wide),
            jax.ShapeDtypeStruct((8, 128), wide),
        ),
        in_specs=[VMEM_WHOLE] * 15,
        out_specs=(VMEM_WHOLE,) * 9,
        scratch_shapes=scratch,
        compiler_params=pltpu.CompilerParams(
            collective_id=0, has_side_effects=True, vmem_limit_bytes=VMEM_BYTES
        ),
    )(x, ids, qkv, qv_bias, out_weight, out_bias, gain1, bias1, up, up_bias, down, down_bias, gain2, bias2, cot)


def outputs_kernel(
    out_in, grad_in, up_full, down_full, query_full, pair_full, out_full, small, shard_sums,
    out, input_grad, g_qkv, g_qv_bias, g_out, g_out_bias, g_gain1, g_bias1, g_up, g_up_bias, g_down, g_down_bias,
    g_gain2, g_bias2,
):
    out[...] = out_in[...]
    input_grad[...] = grad_in[...]
    g_up[...] = flat_rows(up_full).astype(wide)
    g_down[...] = flat_rows(down_full).astype(wide)
    g_qkv[0] = flat_rows(query_full).astype(wide)
    g_qkv[1:] = flat_rows(pair_full).astype(wide).reshape(2, HEAD_DIM, out.shape[1])
    g_out[...] = flat_rows(out_full).astype(wide)
    for i, ref in enumerate((g_out_bias, g_gain1, g_bias1, g_down_bias, g_gain2, g_bias2)):
        ref[...] = small[pl.ds(i, 1)]
    for i in range(2):
        g_up_bias[:, i * 128 : (i + 1) * 128] = shard_sums[pl.ds(i, 1)]
        g_qv_bias[pl.ds(i, 1)] = shard_sums[pl.ds(2, 1), i * HEAD_DIM : (i + 1) * HEAD_DIM]


def write_outputs(results):
    rows, width = results[0].shape
    ff = results[2].shape[2]
    vector = jax.ShapeDtypeStruct((1, width), wide)
    block = jax.ShapeDtypeStruct((rows, width), half)
    return pl.pallas_call(
        outputs_kernel,
        out_shape=(
            block,
            block,
            jax.ShapeDtypeStruct((3, HEAD_DIM, width), wide),
            jax.ShapeDtypeStruct((2, HEAD_DIM), wide),
            jax.ShapeDtypeStruct((HEAD_DIM, width), wide),
            vector,
            vector,
            vector,
            jax.ShapeDtypeStruct((width, ff), wide),
            jax.ShapeDtypeStruct((1, ff), wide),
            jax.ShapeDtypeStruct((ff, width), wide),
            vector,
            vector,
            vector,
        ),
        in_specs=[VMEM_WHOLE] * 9,
        out_specs=(VMEM_WHOLE,) * 14,
    )(*results)


def row(vector):
    return vector.reshape(1, vector.shape[0])


def per_device(
    block_input,
    segment_ids,
    qkv_weight,
    qv_bias,
    out_weight,
    out_bias,
    norm1_gain,
    norm1_bias,
    up_weight,
    up_bias,
    down_weight,
    down_bias,
    norm2_gain,
    norm2_bias,
    cotangent,
):
    results = layer(
        block_input, segment_ids, jnp.swapaxes(qkv_weight, 1, 2), qv_bias, out_weight, row(out_bias),
        row(norm1_gain), row(norm1_bias), up_weight, row(up_bias), down_weight, row(down_bias),
        row(norm2_gain), row(norm2_bias), cotangent,
    )
    out, input_grad, g_qkv, g_qv_bias, g_out, *vectors = write_outputs(results)
    g_out_bias, g_gain1, g_bias1, g_up, g_up_bias, g_down, g_down_bias, g_gain2, g_bias2 = (
        arr.reshape(-1) if arr.shape[0] == 1 else arr for arr in vectors
    )
    return (
        out, input_grad, jnp.swapaxes(g_qkv, 1, 2), g_qv_bias, g_out, g_out_bias, g_gain1, g_bias1,
        g_up, g_up_bias, g_down, g_down_bias, g_gain2, g_bias2,
    )


def solution(mesh):
    placed = (
        P(("dp", "tensor"), None),
        P("dp", None),
        P(None, None, "tensor"),
        P(None, "tensor"),
        P("tensor", None),
        P(),
        P(),
        P(),
        P(None, "tensor"),
        P("tensor"),
        P("tensor", None),
        P(),
        P(),
        P(),
        P(("dp", "tensor"), None),
    )
    return jax.shard_map(
        per_device,
        mesh=mesh,
        in_specs=placed,
        out_specs=(
            P(("dp", "tensor"), None),
            P(("dp", "tensor"), None),
            P(None, None, "tensor"),
            P(None, "tensor"),
            P("tensor", None),
            P(),
            P(),
            P(),
            P(None, "tensor"),
            P("tensor"),
            P("tensor", None),
            P(),
            P(),
            P(),
        ),
        check_vma=False,
    )
```
